128 devices in a mesh: ctx: 32 (over x, z, core), head: 4 (over y).
Axes of the slice: x: 4, y: 4, z: 4, core: 2. Of those that a mesh axis runs over, the one named last changes fastest.
Arguments:
- query_raw: bfloat16 [32768, 2048], P('ctx', 'head'), may hold values from -6 to 6
- key_raw: bfloat16 [32768, 2048], P('ctx', 'head'), may hold values from -6 to 6
- value_raw: bfloat16 [32768, 4096], P('ctx', 'head'), may hold values from -6 to 6
- gate_branch: bfloat16 [32768, 4096], P('ctx', 'head'), may hold values from -6 to 6
- gate_code: int32 [32768, 32], P('ctx', 'head'), may hold values from 0 to 1000
- beta_code: int32 [32768, 32], P('ctx', 'head'), may hold values from 0 to 1000
- conv_query: bfloat16 [4, 2048], P(None, 'head'), may hold values from -3 to 3
- conv_key: bfloat16 [4, 2048], P(None, 'head'), may hold values from -3 to 3
- conv_value: bfloat16 [4, 4096], P(None, 'head'), may hold values from -3 to 3
- norm_gain: float32 [128], replicated, may hold values from 0.1 to 1.9
- out_weight: bfloat16 [4096, 2048], P('head'), may hold values from -0.09375 to 0.09375
Outputs:
- layer_out: bfloat16 [32768, 2048], P(('ctx', 'head'))
The draws below stay inside these ranges and needn't reach their ends.
All inputs are finite; a program needn't handle non-finite values.
Results may differ from the reference program's by a relative error of at most 0.002.
The reference program's roundings to bfloat16 on the way count: a program that leaves them out, or rounds other values in their place, can miss the bound.
Values may be sent and summed in bfloat16 or wider, within the bound.
No kernel may reach another device: no remote copies, remote signals or barrier semaphores. Data moves between devices by JAX's collectives and lax.ppermute only.
A program may use at most 128 MiB of HBM per device.

```python
import jax
import jax.numpy as jnp
from jax import lax

D = 2048
KEY_HEADS = 16
VALUE_HEADS = 32
HEAD_DIM = 128
KERNEL = 4
BLOCK = 64
TOKENS = 32768


def draw_gate_code(key, part):
    level_key = jax.random.fold_in(key, 11)
    order_key = jax.random.fold_in(key, 12)
    token_key = jax.random.fold_in(key, 13)
    ceilings = jax.random.randint(level_key, (VALUE_HEADS,), 0, 1001)
    order = jax.random.permutation(order_key, VALUE_HEADS)
    ceilings = ceilings.at[order[0]].set(1000)
    codes = jax.random.randint(token_key, (TOKENS, VALUE_HEADS), 0, ceilings[None, :] + 1)
    codes = codes.at[0, order[0]].set(1000)
    codes = codes.at[1, order[1]].set(0)
    return codes.astype(jnp.int32)


def plant(array, own_key, smallest, high):
    longest = array.shape.index(max(array.shape))
    spots = []
    for shift in (0, 1):
        where = [jax.random.randint(jax.random.fold_in(own_key, axis), (), 0, length) for axis, length in enumerate(array.shape)]
        where[longest] = (where[longest] + shift) % array.shape[longest]
        spots.append(tuple(where))
    return array.at[spots[0]].set(smallest).at[spots[1]].set(high)


def block_scale(rng, extent, cuts, smallest, top_value):
    factor_of, own = 1.0, jax.random.fold_in(rng, 6)
    for position, parts in cuts:
        heights = jnp.exp(jax.random.uniform(jax.random.fold_in(own, position), (parts,), jnp.float32, smallest / len(cuts), top_value / len(cuts)))
        factor_of = factor_of * jnp.repeat(heights, extent[position] // parts).reshape([-1 if axis == position else 1 for axis in range(len(extent))])
    return factor_of


def centred(own_key, shape, spread, limit, cuts=(), kind=jnp.bfloat16):
    level = block_scale(own_key, shape, cuts, -0.22, 0.18) if cuts else 1.0
    values = jax.random.normal(own_key, shape, jnp.float32) * spread * level
    return jnp.minimum(jnp.maximum(values, -limit), limit).astype(kind)


def setup_inputs(seed: int = 0) -> dict:
    key_of = jax.random.split(jax.random.key(seed), 12)
    return {
        "query_raw": centred(key_of[0], (TOKENS, KEY_HEADS * HEAD_DIM), 1.0, 6.0, ((0, 32), (1, 4))),
        "key_raw": centred(key_of[1], (TOKENS, KEY_HEADS * HEAD_DIM), 1.0, 6.0, ((0, 32), (1, 4))),
        "value_raw": centred(key_of[2], (TOKENS, VALUE_HEADS * HEAD_DIM), 1.0, 6.0, ((0, 32), (1, 4))),
        "gate_branch": centred(key_of[3], (TOKENS, VALUE_HEADS * HEAD_DIM), 1.0, 6.0, ((0, 32), (1, 4))),
        "gate_code": draw_gate_code(jax.random.fold_in(key_of[11], 71), 0),
        "beta_code": plant(jax.random.randint(key_of[5], (TOKENS, VALUE_HEADS), 0, 1001), jax.random.fold_in(key_of[5], 1), 0, 1000).astype(jnp.int32),
        "conv_query": centred(key_of[6], (KERNEL, KEY_HEADS * HEAD_DIM), KERNEL ** -0.5, 3.0, ((1, 4),)),
        "conv_key": centred(key_of[7], (KERNEL, KEY_HEADS * HEAD_DIM), KERNEL ** -0.5, 3.0, ((1, 4),)),
        "conv_value": centred(key_of[8], (KERNEL, VALUE_HEADS * HEAD_DIM), KERNEL ** -0.5, 3.0, ((1, 4),)),
        "norm_gain": jnp.clip(1.0 + 0.18 * jax.random.normal(key_of[9], (HEAD_DIM,), jnp.float32), 0.1, 1.9),
        "out_weight": centred(key_of[10], (VALUE_HEADS * HEAD_DIM, D), (VALUE_HEADS * HEAD_DIM) ** -0.5, 0.09375, ((0, 4),)),
    }


EXACT = lax.Precision.HIGHEST

def causal_conv(earlier, current, weights):
    length = current.shape[0]
    extended = jnp.concatenate([earlier, current], 0).astype(jnp.float32)
    running = jnp.zeros(current.shape, jnp.float32)
    for offset in range(KERNEL):
        running = running + weights[offset].astype(jnp.float32) * extended[offset:offset + length]
    return jax.nn.silu(running)

def unit_rows(values):
    return values * lax.rsqrt(lax.optimization_barrier(jnp.sum(values * values, -1, keepdims=True)) + 1e-06)

def neumann_inverse(strict_part):
    length = strict_part.shape[-1]
    identity = jnp.eye(length, dtype=jnp.float32)
    result = identity - strict_part
    powered = strict_part
    covered = 2
    while covered < length:
        powered = jnp.matmul(powered, powered, precision=EXACT)
        result = jnp.matmul(result, identity + powered, precision=EXACT)
        covered = covered * 2
    return result

def prepare(queries, key_rows, value_rows, log_gate, strength):
    length = queries.shape[-2]
    cumulated = jnp.cumsum(log_gate, axis=-1)
    gap_log = cumulated[..., :, None] - cumulated[..., None, :]
    row_ids = lax.broadcasted_iota(jnp.int32, (length, length), 0)
    col_ids = lax.broadcasted_iota(jnp.int32, (length, length), 1)
    causal_mask = row_ids >= col_ids
    strict_mask = row_ids > col_ids
    decays = jnp.exp(jnp.where(causal_mask, gap_log, 0.0))
    key_dots = jnp.einsum('...id,...jd->...ij', key_rows, key_rows, precision=EXACT)
    strict_part = jnp.where(strict_mask, strength[..., :, None] * key_dots * decays, 0.0)
    inverse = neumann_inverse(strict_part)
    gammas = jnp.exp(cumulated)
    wy_keys = jnp.einsum('...ij,...jd->...id', inverse, (strength * gammas)[..., None] * key_rows, precision=EXACT)
    wy_values = jnp.einsum('...ij,...jd->...id', inverse, strength[..., None] * value_rows, precision=EXACT)
    query_dots = jnp.einsum('...id,...jd->...ij', queries, key_rows, precision=EXACT)
    mixing = jnp.where(causal_mask, query_dots * decays, 0.0)
    key_tails = jnp.exp(cumulated[..., -1:] - cumulated)[..., None] * key_rows
    block_decay = jnp.exp(cumulated[..., -1])
    return (gammas, mixing, wy_keys, wy_values, key_tails, block_decay)

def gated_norm(emitted, branch, gain_vector):
    scaled = emitted * lax.rsqrt(lax.optimization_barrier(jnp.mean(emitted * emitted, -1, keepdims=True)) + 1e-06) * gain_vector
    gating = jax.nn.silu(branch.astype(jnp.float32)).reshape(emitted.shape)
    return (scaled * gating).reshape(emitted.shape[0], -1).astype(jnp.bfloat16)

def reference(query_raw, key_raw, value_raw, gate_branch, gate_code, beta_code, conv_query, conv_key, conv_value, norm_gain, out_weight):
    group_ratio = VALUE_HEADS // KEY_HEADS
    blocks = TOKENS // BLOCK
    margin = KERNEL - 1

    def regroup(source):
        return source.reshape((blocks, BLOCK) + source.shape[1:])
    inputs = (regroup(query_raw), regroup(key_raw), regroup(value_raw), regroup(gate_branch), regroup(gate_code), regroup(beta_code))
    start_state = jnp.zeros((VALUE_HEADS, HEAD_DIM, HEAD_DIM), jnp.float32)
    start_rims = (jnp.zeros((margin, query_raw.shape[1]), query_raw.dtype), jnp.zeros((margin, key_raw.shape[1]), key_raw.dtype), jnp.zeros((margin, value_raw.shape[1]), value_raw.dtype))

    def advance(loop_carry, pieces):
        carried, rim_rows = loop_carry
        query_piece, key_piece, value_piece, branch_piece, code_piece, beta_piece = pieces
        query_conv = causal_conv(rim_rows[0], query_piece, conv_query)
        key_conv = causal_conv(rim_rows[1], key_piece, conv_key)
        value_conv = causal_conv(rim_rows[2], value_piece, conv_value)
        queries = unit_rows(query_conv.reshape(BLOCK, KEY_HEADS, HEAD_DIM)) * HEAD_DIM ** (-0.5)
        key_rows = unit_rows(key_conv.reshape(BLOCK, KEY_HEADS, HEAD_DIM))
        queries = jnp.repeat(queries, group_ratio, axis=1).transpose(1, 0, 2)
        key_rows = jnp.repeat(key_rows, group_ratio, axis=1).transpose(1, 0, 2)
        value_rows = value_conv.reshape(BLOCK, VALUE_HEADS, HEAD_DIM).transpose(1, 0, 2)
        log_gate = jnp.log1p(-1e-06 * code_piece.astype(jnp.float32)).T
        strength = (beta_piece.astype(jnp.float32) / 1000.0).T
        gammas, mixing, wy_keys, wy_values, key_tails, block_decay = prepare(queries, key_rows, value_rows, log_gate, strength)
        fresh = wy_values - jnp.einsum('hid,hde->hie', wy_keys, carried, precision=EXACT)
        emitted = gammas[..., None] * jnp.einsum('hid,hde->hie', queries, carried, precision=EXACT)
        emitted = emitted + jnp.einsum('hij,hje->hie', mixing, fresh, precision=EXACT)
        carried = block_decay[:, None, None] * carried + jnp.einsum('hid,hie->hde', key_tails, fresh, precision=EXACT)
        normed = gated_norm(emitted.transpose(1, 0, 2), branch_piece, norm_gain)
        mixed_rows = jnp.dot(normed, out_weight, preferred_element_type=jnp.float32).astype(jnp.bfloat16)
        new_rims = (query_piece[BLOCK - margin:], key_piece[BLOCK - margin:], value_piece[BLOCK - margin:])
        return ((carried, new_rims), mixed_rows)
    _, outputs = lax.scan(advance, (start_state, start_rims), inputs)
    return outputs.reshape(TOKENS, D)
```

```python
import jax, jax.numpy as jnp
from jax import lax
from jax.experimental import pallas as pl
from jax.experimental.pallas import tpu as pltpu
from jax.sharding import PartitionSpec as P

Z_CHIPS, X_CHIPS, CORES = 4, 4, 2

F32, BF16 = jnp.float32, jnp.bfloat16
HD = 128
BLOCK = 64
KERNEL = 4


def split(x):
    hi = x.astype(BF16)
    return hi, (x - hi.astype(F32)).astype(BF16)


def mxu(a, b):
    return jnp.dot(a, b, preferred_element_type=F32)


def cat(parts, axis):
    return jnp.concatenate(parts, axis)


def silu(x):
    return x / (1.0 + jnp.exp(-x))


def pair_rhs(y, left):
    hi, lo = split(y)
    zero = jnp.zeros_like(hi)
    hi = cat([jnp.where(left, hi, zero), jnp.where(left, zero, hi)], 0)
    lo = cat([jnp.where(left, lo, zero), jnp.where(left, zero, lo)], 0)
    row = cat([hi, lo], 1)
    return cat([row, row], 0)


def wide(x):
    return cat(split(x), 1)


def fold(out):
    return out[:, :HD] + out[:, HD:]


def pair_inverse(low, eye, left):
    inv = eye - low
    power = fold(mxu(wide(low), pair_rhs(low, left)))
    covered = 4
    while covered < BLOCK:
        out = fold(mxu(wide(cat([inv, power], 0)), pair_rhs(power, left)))
        inv = inv + out[:BLOCK]
        power = out[BLOCK:]
        covered *= 2
    return inv + fold(mxu(wide(inv), pair_rhs(power, left)))


def conv(ext, taps):
    acc = None
    for j in range(KERNEL):
        s = KERNEL - 1 - j
        shifted = ext if s == 0 else pltpu.roll(ext, s, 0)
        term = taps[j : j + 1] * shifted[8:]
        acc = term if acc is None else acc + term
    return silu(acc)


def unit(x):
    return x * lax.rsqrt(jnp.sum(x * x, -1, keepdims=True) + 1e-06)


def scan_kernel(q_ref, k_ref, v_ref, gc_ref, bc_ref, halo_ref, cq_ref, ck_ref, cv_ref,
                base_ref, map_ref, fin_ref, state, carry):
    n = pl.program_id(0)
    kh = q_ref.shape[1] // HD
    vh = v_ref.shape[1] // HD
    kw, vw = kh * HD, vh * HD

    @pl.when(n == 0)
    def _():
        carry[...] = halo_ref[...].astype(F32)
        r = lax.broadcasted_iota(jnp.int32, (HD, 2 * HD), 0)
        c = lax.broadcasted_iota(jnp.int32, (HD, 2 * HD), 1)
        start = jnp.where(r + HD == c, 1.0, 0.0).astype(F32)
        for h in range(vh):
            state[h] = start

    rows = lax.broadcasted_iota(jnp.int32, (BLOCK, HD), 0)
    lanes = lax.broadcasted_iota(jnp.int32, (BLOCK, HD), 1)
    left = lanes < BLOCK
    cols = jnp.where(left, lanes, lanes - BLOCK)
    left16 = left
    causal = rows >= cols
    strict = rows > cols
    eye = jnp.where(rows == cols, 1.0, 0.0).astype(F32)
    left_t = lax.broadcasted_iota(jnp.int32, (HD, HD), 1) < BLOCK

    log_gate = jnp.log1p(-1e-06 * gc_ref[...].astype(F32))
    tri = jnp.where(causal, 1.0, 0.0).astype(F32)[:, :BLOCK]
    cum = jnp.dot(tri, log_gate, precision=lax.Precision.HIGHEST, preferred_element_type=F32)
    gamma = jnp.exp(cum)
    beta = bc_ref[...].astype(F32) / 1000.0
    beta_g = beta * jnp.exp(-cum)
    last = gamma[BLOCK - 1 :]

    for j in range(kh):
        def conved(ref, taps, off, width):
            x = ref[...].astype(F32)
            ext = cat([carry[:, off : off + width], x], 0)
            out = conv(ext, taps)
            return out, x[BLOCK - 8 :]
        sl = slice(j * HD, (j + 1) * HD)
        qx, qtail = conved(q_ref.at[:, sl], cq_ref[:, sl], j * HD, HD)
        kx, ktail = conved(k_ref.at[:, sl], ck_ref[:, sl], kw + j * HD, HD)
        vs = slice(2 * j * HD, 2 * (j + 1) * HD)
        vx, vtail = conved(v_ref.at[:, vs], cv_ref[:, vs], 2 * kw + 2 * j * HD, 2 * HD)
        carry[:, j * HD : (j + 1) * HD] = qtail
        carry[:, kw + j * HD : kw + (j + 1) * HD] = ktail
        carry[:, 2 * kw + 2 * j * HD : 2 * kw + 2 * (j + 1) * HD] = vtail
        q = unit(qx) * HD ** (-0.5)
        k = unit(kx)
        kq = cat([k, q], 0)
        kq_hi, kq_lo = split(kq)
        kt = jnp.transpose(cat([k, k], 0))
        kt_hi, kt_lo = split(kt)
        kt_row = cat([kt_hi, kt_lo], 1)
        dots = fold(mxu(cat([kq_hi, kq_lo], 1), cat([kt_row, kt_row], 0)))
        b0 = jnp.broadcast_to(beta[:, 2 * j : 2 * j + 1], (BLOCK, HD))
        b1 = jnp.broadcast_to(beta[:, 2 * j + 1 : 2 * j + 2], (BLOCK, HD))
        low = jnp.where(strict, jnp.where(left, b0, b1) * dots[:BLOCK], 0.0)
        mix = jnp.where(causal, dots[BLOCK:], 0.0)
        inv = pair_inverse(low, eye, left16)
        ih, il = split(inv)
        rh, rl = split(pltpu.roll(inv, BLOCK, 1))
        t0 = jnp.where(left16, ih, rl)
        t1 = jnp.where(left16, rh, il)
        mh, ml = split(mix)
        m2 = jnp.where(left16, mh, ml)
        k2 = jnp.where(left_t, kt_hi, kt_lo)
        km = cat([k2, m2], 0)
        km4 = cat([km, km], 1)
        kq3 = cat([kq_hi, kq_lo, kq_hi], 1)
        for a, (t, b) in enumerate(((t0, b0), (t1, b1))):
            h = 2 * j + a
            s = state[h]
            s_hi, s_lo = split(s)
            z = mxu(kq3, cat([s_hi, s_hi, s_lo], 0))
            bg = beta_g[:, h : h + 1]
            right = cat([bg * vx[:, a * HD : (a + 1) * HD] - b * z[:BLOCK, :HD], -b * z[:BLOCK, HD:]], 1)
            r_hi, r_lo = split(right)
            u = mxu(cat([t, t], 1), cat([r_hi, r_hi, r_lo, r_lo], 0))
            u_hi, u_lo = split(u)
            ds = mxu(km4, cat([u_hi, u_hi, u_lo, u_lo], 0))
            g = gamma[:, h : h + 1]
            o = g * (z[BLOCK:] + ds[HD:])
            state[h] = last[:, h : h + 1] * (s + ds[:HD])
            base_ref[:, h * HD : (h + 1) * HD] = o[:, :HD]
            o_hi, o_lo = split(o[:, HD:])
            map_ref[:, 2 * h * HD : (2 * h + 1) * HD] = o_hi
            map_ref[:, (2 * h + 1) * HD : (2 * h + 2) * HD] = o_lo

    @pl.when(n == pl.num_programs(0) - 1)
    def _():
        fin_ref[...] = state[...]


def run_scan(q, k, v, gc, bc, halo, cq, ck, cv):
    rows = q.shape[0]
    kw, vw = q.shape[1], v.shape[1]
    vh = vw // HD
    row_spec = lambda w: pl.BlockSpec((BLOCK, w), lambda n: (n, 0))
    full = lambda a: pl.BlockSpec(a.shape, lambda n: (0,) * a.ndim)
    return pl.pallas_call(
        scan_kernel,
        grid=(rows // BLOCK,),
        in_specs=[row_spec(kw), row_spec(kw), row_spec(vw), row_spec(vh), row_spec(vh),
                  full(halo), full(cq), full(ck), full(cv)],
        out_specs=[row_spec(vw), row_spec(2 * vw), pl.BlockSpec((vh, HD, 2 * HD), lambda n: (0, 0, 0))],
        out_shape=[jax.ShapeDtypeStruct((rows, vw), F32),
                   jax.ShapeDtypeStruct((rows, 2 * vw), BF16),
                   jax.ShapeDtypeStruct((vh, HD, 2 * HD), F32)],
        scratch_shapes=[pltpu.VMEM((vh, HD, 2 * HD), F32), pltpu.VMEM((8, 2 * kw + vw), F32)],
        compiler_params=pltpu.CompilerParams(dimension_semantics=("arbitrary",), vmem_limit_bytes=56 << 20),
        name="scan",
    )(q, k, v, gc, bc, halo, cq.astype(F32), ck.astype(F32), cv.astype(F32))


def dot3(a, b):
    a_hi, a_lo = split(a)
    b_hi, b_lo = split(b)
    return mxu(cat([a_hi, a_lo, a_hi], 1), cat([b_hi, b_hi, b_lo], 0))


def then(later, earlier):
    out = dot3(later[:, HD:], earlier)
    return cat([later[:, :HD] + out[:, :HD], out[:, HD:]], 1)


def vmem_call(body, outs, scratch, name, scalars, *arrays):
    return pl.pallas_call(
        body,
        in_specs=[pl.BlockSpec(memory_space=pltpu.SMEM)] + [pl.BlockSpec(memory_space=pltpu.VMEM)] * len(arrays),
        out_specs=[pl.BlockSpec(memory_space=pltpu.VMEM)] * len(outs),
        out_shape=[jax.ShapeDtypeStruct(s, F32) for s in outs],
        scratch_shapes=[pltpu.VMEM(s, F32) for s in scratch],
        name=name,
    )(scalars, *arrays)


def pair_kernel(pos, kept, got, early_ref, both_ref):
    first = pos[2] == 0
    for h in range(kept.shape[0]):
        mine, other = kept[h], got[h]
        early = jnp.where(first, mine, other)
        late = jnp.where(first, other, mine)
        early_ref[h] = early
        both_ref[h] = then(late, early)


def prefix_kernel(pos, a0, a1, a2, a3, pre_ref, tot_ref, line):
    z = pos[1]
    for d, a in enumerate((a0, a1, a2, a3)):
        line[(z - d + Z_CHIPS) % Z_CHIPS] = a[...]
    r = lax.broadcasted_iota(jnp.int32, (HD, 2 * HD), 0)
    c = lax.broadcasted_iota(jnp.int32, (HD, 2 * HD), 1)
    pre_ref[0] = jnp.where(r + HD == c, 1.0, 0.0).astype(F32)
    run = line[0]
    for i in range(1, Z_CHIPS):
        pre_ref[i] = run
        run = then(line[i], run)
    tot_ref[...] = run


def entry_kernel(pos, a0, a1, a2, a3, pre, out_ref, line, states):
    x = pos[0]
    for d, a in enumerate((a0, a1, a2, a3)):
        line[(x - d + X_CHIPS) % X_CHIPS] = a[...]
    run = jnp.zeros((HD, HD), F32)
    for i in range(X_CHIPS):
        states[i] = run
        if i + 1 < X_CHIPS:
            run = line[i, :, :HD] + dot3(line[i, :, HD:], run)
    mine = states[x]
    out_ref[0] = mine
    for i in range(1, Z_CHIPS):
        out_ref[i] = pre[i, :, :HD] + dot3(pre[i, :, HD:], mine)


def cores_kernel(pos, a0, a1, a2, a3, early, keep_ref, send_ref, line):
    z, first = pos[1], pos[2] == 0
    for d, a in enumerate((a0, a1, a2, a3)):
        line[(z - d + Z_CHIPS) % Z_CHIPS] = a[...]
    for h in range(Z_CHIPS):
        s = line[h]
        t = early[h, :, :HD] + dot3(early[h, :, HD:], s)
        keep_ref[h] = jnp.where(first, s, t)
        send_ref[h] = jnp.where(first, t, s)


def out_kernel(pos, base_ref, map_ref, kept, got, gate_ref, gain_ref, y_ref):
    h = pl.program_id(0)
    per = kept.shape[0]
    own = (h // per) == pos[2]
    s = jnp.where(own, kept[h % per], got[h % per])
    row = wide(s)
    o = base_ref[...] + fold(mxu(map_ref[...], cat([row, row], 0)))
    g = gate_ref[...].astype(F32)
    y = o * lax.rsqrt(jnp.mean(o * o, -1, keepdims=True) + 1e-06) * gain_ref[...] * silu(g)
    y_ref[...] = y.astype(BF16)


def run_out(pos, base, maps, kept, got, gate, gain):
    rows, width = base.shape
    col = lambda w: pl.BlockSpec((rows, w), lambda h: (0, h))
    full = lambda a: pl.BlockSpec(a.shape, lambda h: (0,) * a.ndim)
    return pl.pallas_call(
        out_kernel,
        grid=(width // HD,),
        in_specs=[pl.BlockSpec(memory_space=pltpu.SMEM), col(HD), col(2 * HD), full(kept), full(got), col(HD), full(gain)],
        out_specs=col(HD),
        out_shape=jax.ShapeDtypeStruct((rows, width), BF16),
        name="out",
    )(pos, base, maps, kept, got, gate, gain)


def ctx_route(dx, dz, dc):
    def dest(i):
        x, z, c = i // (Z_CHIPS * CORES), (i // CORES) % Z_CHIPS, i % CORES
        return ((x + dx) % X_CHIPS * Z_CHIPS + (z + dz) % Z_CHIPS) * CORES + (c + dc) % CORES
    return [(i, dest(i)) for i in range(X_CHIPS * Z_CHIPS * CORES)]


def row_of(array, index):
    return lax.dynamic_index_in_dim(array, index, 0, keepdims=False)


def shards(query_raw, key_raw, value_raw, gate_branch, gate_code, beta_code,
           conv_query, conv_key, conv_value, norm_gain, out_weight):
    tok_rows = query_raw.shape[0]
    vh = value_raw.shape[1] // HD
    half = vh // CORES
    ctx = lax.axis_index("ctx")
    head = lax.axis_index("head")
    heads = lax.axis_size("head")
    x, z, core = ctx // (Z_CHIPS * CORES), (ctx // CORES) % Z_CHIPS, ctx % CORES
    pos = jnp.stack([x, z, core]).astype(jnp.int32)
    send = lambda a, dx, dz, dc: lax.ppermute(a, "ctx", ctx_route(dx, dz, dc))
    turn = lambda a, d: lax.ppermute(a, "head", [(i, (i + d) % heads) for i in range(heads)])

    rim = cat([a[tok_rows - 8 :] for a in (query_raw, key_raw, value_raw)], 1)
    n_ctx = lax.axis_size("ctx")
    halo = lax.ppermute(rim, "ctx", [(i, i + 1) for i in range(n_ctx - 1)])

    w_rows = out_weight.shape[0] // CORES
    w_mine = lax.dynamic_slice_in_dim(out_weight, core * w_rows, w_rows, 0)
    w_got = [turn(w_mine, d) for d in range(1, heads)]

    base, maps, fin = run_scan(query_raw, key_raw, value_raw, gate_code, beta_code, halo,
                               conv_query, conv_key, conv_value)

    kept = lax.dynamic_slice_in_dim(fin, core * half, half, 0)
    away = lax.dynamic_slice_in_dim(fin, (1 - core) * half, half, 0)
    early, both = vmem_call(pair_kernel, [kept.shape] * 2, [], "pair", pos, kept, send(away, 0, 0, 1))
    lines = [row_of(both, z)] + [send(row_of(both, (z + d) % Z_CHIPS), 0, d, 0) for d in range(1, Z_CHIPS)]
    pre, tot = vmem_call(prefix_kernel, [(Z_CHIPS, HD, 2 * HD), (HD, 2 * HD)], [(Z_CHIPS, HD, 2 * HD)],
                         "prefix", pos, *lines)
    tots = [tot] + [send(tot, d, 0, 0) for d in range(1, X_CHIPS)]
    entry, = vmem_call(entry_kernel, [(Z_CHIPS, HD, HD)], [(X_CHIPS, HD, 2 * HD), (X_CHIPS, HD, HD)],
                       "entry", pos, *tots, pre)
    backs = [row_of(entry, z)] + [send(row_of(entry, (z + d) % Z_CHIPS), 0, d, 0) for d in range(1, Z_CHIPS)]
    own, lent = vmem_call(cores_kernel, [(half, HD, HD)] * 2, [(Z_CHIPS, HD, HD)], "cores", pos, *backs, early)
    got = send(lent, 0, 0, 1)

    w_other = [send(w, 0, 0, 1) for w in w_got]

    y = run_out(pos, base, maps, own, got, gate_branch, norm_gain.reshape(1, HD))
    rows = tok_rows // heads
    piece = lambda i: lax.dynamic_slice_in_dim(y, i * rows, rows, 0)
    y_got = [turn(piece((head + d) % heads), d) for d in range(1, heads)]
    total = jnp.dot(piece(head), out_weight, preferred_element_type=F32)
    for yd, wm, wo in zip(y_got, w_got, w_other):
        w = jnp.where(core == 0, cat([wm, wo], 0), cat([wo, wm], 0))
        total = total + jnp.dot(yd, w, preferred_element_type=F32)
    return total.astype(BF16)


def solution(mesh):
    return jax.shard_map(
        shards,
        mesh=mesh,
        in_specs=(P("ctx", "head"),) * 6 + (P(None, "head"),) * 3 + (P(), P("head", None)),
        out_specs=P(("ctx", "head"), None),
        check_vma=False,
    )
```

```python
import jax, jax.numpy as jnp
from jax import lax
from jax.experimental import pallas as pl
from jax.experimental.pallas import tpu as pltpu
from jax.sharding import PartitionSpec as P

Z_CHIPS, X_CHIPS, CORES = 4, 4, 2

F32, BF16 = jnp.float32, jnp.bfloat16
HD = 128
BLOCK = 64
KERNEL = 4


def split(x):
    hi = x.astype(BF16)
    return hi, (x - hi.astype(F32)).astype(BF16)


def mxu(a, b):
    return jnp.dot(a, b, preferred_element_type=F32)


def cat(parts, axis):
    return jnp.concatenate(parts, axis)


def silu(x):
    return x / (1.0 + jnp.exp(-x))


def pair_rhs(y, left):
    hi, lo = split(y)
    zero = jnp.zeros_like(hi)
    hi = cat([jnp.where(left, hi, zero), jnp.where(left, zero, hi)], 0)
    lo = cat([jnp.where(left, lo, zero), jnp.where(left, zero, lo)], 0)
    row = cat([hi, lo], 1)
    return cat([row, row], 0)


def wide(x):
    return cat(split(x), 1)


def fold(out):
    return out[:, :HD] + out[:, HD:]


def pair_inverses(lows, eye, left, fills):
    raw = [mxu(wide(low), pair_rhs(low, left)) for low in lows]
    fills[0]()
    powers = [fold(r) for r in raw]
    invs = [eye - low for low in lows]
    for fill in fills[1:-1]:
        raw = [mxu(wide(cat([i, p], 0)), pair_rhs(p, left)) for i, p in zip(invs, powers)]
        fill()
        outs = [fold(r) for r in raw]
        invs = [i + o[:BLOCK] for i, o in zip(invs, outs)]
        powers = [o[BLOCK:] for o in outs]
    raw = [mxu(wide(i), pair_rhs(p, left)) for i, p in zip(invs, powers)]
    fills[-1]()
    return [i + fold(r) for i, r in zip(invs, raw)]


def conv(ext, taps):
    acc = None
    for j in range(KERNEL):
        s = KERNEL - 1 - j
        shifted = ext if s == 0 else pltpu.roll(ext, s, 0)
        term = taps[j : j + 1] * shifted[8:]
        acc = term if acc is None else acc + term
    return silu(acc)


def unit(x):
    return x * lax.rsqrt(jnp.sum(x * x, -1, keepdims=True) + 1e-06)


def scan_kernel(q_ref, k_ref, v_ref, gc_ref, bc_ref, halo_ref, cq_ref, ck_ref, cv_ref,
                base_ref, map_ref, fin_ref, state, carry):
    n = pl.program_id(0)
    kh = q_ref.shape[1] // HD
    vh = v_ref.shape[1] // HD
    kw, vw = kh * HD, vh * HD

    @pl.when(n == 0)
    def _():
        carry[...] = halo_ref[...].astype(F32)
        r = lax.broadcasted_iota(jnp.int32, (HD, 2 * HD), 0)
        c = lax.broadcasted_iota(jnp.int32, (HD, 2 * HD), 1)
        start = jnp.where(r + HD == c, 1.0, 0.0).astype(F32)
        for h in range(vh):
            state[h] = start

    rows = lax.broadcasted_iota(jnp.int32, (BLOCK, HD), 0)
    lanes = lax.broadcasted_iota(jnp.int32, (BLOCK, HD), 1)
    left = lanes < BLOCK
    cols = jnp.where(left, lanes, lanes - BLOCK)
    causal = rows >= cols
    strict = rows > cols
    eye = jnp.where(rows == cols, 1.0, 0.0).astype(F32)
    left_t = lax.broadcasted_iota(jnp.int32, (HD, HD), 1) < BLOCK

    log_gate = jnp.log1p(-1e-06 * gc_ref[...].astype(F32))
    tri = jnp.where(causal, 1.0, 0.0).astype(F32)[:, :BLOCK]
    cum = jnp.dot(tri, log_gate, precision=lax.Precision.HIGHEST, preferred_element_type=F32)
    gamma = jnp.exp(cum)
    beta = bc_ref[...].astype(F32) / 1000.0
    beta_g = beta * jnp.exp(-cum)
    last = gamma[BLOCK - 1 :]

    def conved(ref, taps, src, dst, width):
        x = ref[:, src : src + width].astype(F32)
        ext = cat([carry[:, dst : dst + width], x], 0)
        carry[:, dst : dst + width] = x[BLOCK - 8 :]
        return conv(ext, taps[:, src : src + width])

    pairs = range(kh)
    each = range(vh)
    bs = [jnp.broadcast_to(beta[:, h : h + 1], (BLOCK, HD)) for h in each]
    kt2, k2, q2, lows = [], [], [None] * kh, []
    for j in pairs:
        k = unit(conved(k_ref, ck_ref, j * HD, kw + j * HD, HD))
        kt_hi, kt_lo = split(jnp.transpose(cat([k, k], 0)))
        kt2.append((kt_hi, kt_lo))
        k2.append(wide(k))
    for j in pairs:
        row = cat(kt2[j], 1)
        dots = fold(mxu(k2[j], cat([row, row], 0)))
        lows.append(jnp.where(strict, jnp.where(left, bs[2 * j], bs[2 * j + 1]) * dots, 0.0))
    km4, zs, vs = [None] * kh, [None] * vh, [None] * vh

    def fill_q(js):
        for j in js:
            q2[j] = wide(unit(conved(q_ref, cq_ref, j * HD, j * HD, HD)) * HD ** (-0.5))

    def fill_mix(js):
        for j in js:
            row = cat(kt2[j], 1)
            dots = fold(mxu(q2[j], cat([row, row], 0)))
            mh, ml = split(jnp.where(causal, dots, 0.0))
            km = cat([jnp.where(left_t, *kt2[j]), jnp.where(left, mh, ml)], 0)
            km4[j] = cat([km, km], 1)

    def fill_v(hs):
        for h in hs:
            vs[h] = beta_g[:, h : h + 1] * conved(v_ref, cv_ref, h * HD, 2 * kw + h * HD, HD)

    def fill_z(hs):
        for h in hs:
            s_hi, s_lo = split(state[h])
            kq = cat([k2[h // 2], q2[h // 2]], 0)
            zs[h] = mxu(cat([kq, kq[:, :HD]], 1), cat([s_hi, s_hi, s_lo], 0))

    half = vh // 2
    fills = [lambda: fill_q(pairs[: kh // 2]), lambda: fill_q(pairs[kh // 2 :]), lambda: fill_mix(pairs),
             lambda: fill_v(each[:half]), lambda: fill_v(each[half:]), lambda: fill_z(each)]
    invs = pair_inverses(lows, eye, left, fills)
    ts = []
    for inv in invs:
        ih, il = split(inv)
        rh, rl = split(pltpu.roll(inv, BLOCK, 1))
        for t in (jnp.where(left, ih, rl), jnp.where(left, rh, il)):
            ts.append(cat([t, t], 1))
    us = []
    for h in each:
        z = zs[h]
        right = cat([vs[h] - bs[h] * z[:BLOCK, :HD], -bs[h] * z[:BLOCK, HD:]], 1)
        r_hi, r_lo = split(right)
        us.append(mxu(ts[h], cat([r_hi, r_hi, r_lo, r_lo], 0)))
    for h in each:
        u_hi, u_lo = split(us[h])
        ds = mxu(km4[h // 2], cat([u_hi, u_hi, u_lo, u_lo], 0))
        o = gamma[:, h : h + 1] * (zs[h][BLOCK:] + ds[HD:])
        state[h] = last[:, h : h + 1] * (state[h] + ds[:HD])
        base_ref[:, h * HD : (h + 1) * HD] = o[:, :HD]
        o_hi, o_lo = split(o[:, HD:])
        map_ref[:, 2 * h * HD : (2 * h + 1) * HD] = o_hi
        map_ref[:, (2 * h + 1) * HD : (2 * h + 2) * HD] = o_lo

    @pl.when(n == pl.num_programs(0) - 1)
    def _():
        fin_ref[...] = state[...]


def run_scan(q, k, v, gc, bc, halo, cq, ck, cv):
    rows = q.shape[0]
    kw, vw = q.shape[1], v.shape[1]
    vh = vw // HD
    row_spec = lambda w: pl.BlockSpec((BLOCK, w), lambda n: (n, 0))
    full = lambda a: pl.BlockSpec(a.shape, lambda n: (0,) * a.ndim)
    return pl.pallas_call(
        scan_kernel,
        grid=(rows // BLOCK,),
        in_specs=[row_spec(kw), row_spec(kw), row_spec(vw), row_spec(vh), row_spec(vh),
                  full(halo), full(cq), full(ck), full(cv)],
        out_specs=[row_spec(vw), row_spec(2 * vw), pl.BlockSpec((vh, HD, 2 * HD), lambda n: (0, 0, 0))],
        out_shape=[jax.ShapeDtypeStruct((rows, vw), F32),
                   jax.ShapeDtypeStruct((rows, 2 * vw), BF16),
                   jax.ShapeDtypeStruct((vh, HD, 2 * HD), F32)],
        scratch_shapes=[pltpu.VMEM((vh, HD, 2 * HD), F32), pltpu.VMEM((8, 2 * kw + vw), F32)],
        compiler_params=pltpu.CompilerParams(dimension_semantics=("arbitrary",), vmem_limit_bytes=56 << 20),
        name="scan",
    )(q, k, v, gc, bc, halo, cq.astype(F32), ck.astype(F32), cv.astype(F32))


def dot3(a, b):
    a_hi, a_lo = split(a)
    b_hi, b_lo = split(b)
    return mxu(cat([a_hi, a_lo, a_hi], 1), cat([b_hi, b_hi, b_lo], 0))


def then(later, earlier):
    out = dot3(later[:, HD:], earlier)
    return cat([later[:, :HD] + out[:, :HD], out[:, HD:]], 1)


def vmem_call(body, outs, scratch, name, scalars, *arrays):
    return pl.pallas_call(
        body,
        in_specs=[pl.BlockSpec(memory_space=pltpu.SMEM)] + [pl.BlockSpec(memory_space=pltpu.VMEM)] * len(arrays),
        out_specs=[pl.BlockSpec(memory_space=pltpu.VMEM)] * len(outs),
        out_shape=[jax.ShapeDtypeStruct(s, F32) for s in outs],
        scratch_shapes=[pltpu.VMEM(s, F32) for s in scratch],
        name=name,
    )(scalars, *arrays)


def pair_kernel(pos, kept, got, early_ref, both_ref):
    first = pos[2] == 0
    for h in range(kept.shape[0]):
        mine, other = kept[h], got[h]
        early = jnp.where(first, mine, other)
        late = jnp.where(first, other, mine)
        early_ref[h] = early
        both_ref[h] = then(late, early)


def prefix_kernel(pos, a0, a1, a2, a3, pre_ref, tot_ref, line):
    z = pos[1]
    for d, a in enumerate((a0, a1, a2, a3)):
        line[(z - d + Z_CHIPS) % Z_CHIPS] = a[...]
    r = lax.broadcasted_iota(jnp.int32, (HD, 2 * HD), 0)
    c = lax.broadcasted_iota(jnp.int32, (HD, 2 * HD), 1)
    pre_ref[0] = jnp.where(r + HD == c, 1.0, 0.0).astype(F32)
    run = line[0]
    for i in range(1, Z_CHIPS):
        pre_ref[i] = run
        run = then(line[i], run)
    tot_ref[...] = run


def entry_kernel(pos, a0, a1, a2, a3, pre, out_ref, line, states):
    x = pos[0]
    for d, a in enumerate((a0, a1, a2, a3)):
        line[(x - d + X_CHIPS) % X_CHIPS] = a[...]
    run = jnp.zeros((HD, HD), F32)
    for i in range(X_CHIPS):
        states[i] = run
        if i + 1 < X_CHIPS:
            run = line[i, :, :HD] + dot3(line[i, :, HD:], run)
    mine = states[x]
    out_ref[0] = mine
    for i in range(1, Z_CHIPS):
        out_ref[i] = pre[i, :, :HD] + dot3(pre[i, :, HD:], mine)


def cores_kernel(pos, a0, a1, a2, a3, early, keep_ref, send_ref, line):
    z, first = pos[1], pos[2] == 0
    for d, a in enumerate((a0, a1, a2, a3)):
        line[(z - d + Z_CHIPS) % Z_CHIPS] = a[...]
    for h in range(Z_CHIPS):
        s = line[h]
        t = early[h, :, :HD] + dot3(early[h, :, HD:], s)
        keep_ref[h] = jnp.where(first, s, t)
        send_ref[h] = jnp.where(first, t, s)


def out_kernel(pos, base_ref, map_ref, kept, got, gate_ref, gain_ref, y_ref):
    h = pl.program_id(0)
    per = kept.shape[0]
    own = (h // per) == pos[2]
    s = jnp.where(own, kept[h % per], got[h % per])
    row = wide(s)
    o = base_ref[...] + fold(mxu(map_ref[...], cat([row, row], 0)))
    g = gate_ref[...].astype(F32)
    y = o * lax.rsqrt(jnp.mean(o * o, -1, keepdims=True) + 1e-06) * gain_ref[...] * silu(g)
    y_ref[...] = y.astype(BF16)


def run_out(pos, base, maps, kept, got, gate, gain):
    rows, width = base.shape
    col = lambda w: pl.BlockSpec((rows, w), lambda h: (0, h))
    full = lambda a: pl.BlockSpec(a.shape, lambda h: (0,) * a.ndim)
    return pl.pallas_call(
        out_kernel,
        grid=(width // HD,),
        in_specs=[pl.BlockSpec(memory_space=pltpu.SMEM), col(HD), col(2 * HD), full(kept), full(got), col(HD), full(gain)],
        out_specs=col(HD),
        out_shape=jax.ShapeDtypeStruct((rows, width), BF16),
        name="out",
    )(pos, base, maps, kept, got, gate, gain)


def ctx_route(dx, dz, dc):
    def dest(i):
        x, z, c = i // (Z_CHIPS * CORES), (i // CORES) % Z_CHIPS, i % CORES
        return ((x + dx) % X_CHIPS * Z_CHIPS + (z + dz) % Z_CHIPS) * CORES + (c + dc) % CORES
    return [(i, dest(i)) for i in range(X_CHIPS * Z_CHIPS * CORES)]


def row_of(array, index):
    return lax.dynamic_index_in_dim(array, index, 0, keepdims=False)


def shards(query_raw, key_raw, value_raw, gate_branch, gate_code, beta_code,
           conv_query, conv_key, conv_value, norm_gain, out_weight):
    tok_rows = query_raw.shape[0]
    vh = value_raw.shape[1] // HD
    half = vh // CORES
    ctx = lax.axis_index("ctx")
    head = lax.axis_index("head")
    heads = lax.axis_size("head")
    x, z, core = ctx // (Z_CHIPS * CORES), (ctx // CORES) % Z_CHIPS, ctx % CORES
    pos = jnp.stack([x, z, core]).astype(jnp.int32)
    send = lambda a, dx, dz, dc: lax.ppermute(a, "ctx", ctx_route(dx, dz, dc))
    turn = lambda a, d: lax.ppermute(a, "head", [(i, (i + d) % heads) for i in range(heads)])

    rim = cat([a[tok_rows - 8 :] for a in (query_raw, key_raw, value_raw)], 1)
    n_ctx = lax.axis_size("ctx")
    halo = lax.ppermute(rim, "ctx", [(i, i + 1) for i in range(n_ctx - 1)])

    w_rows = out_weight.shape[0] // CORES
    w_mine = lax.dynamic_slice_in_dim(out_weight, core * w_rows, w_rows, 0)
    w_got = [turn(w_mine, d) for d in range(1, heads)]

    base, maps, fin = run_scan(query_raw, key_raw, value_raw, gate_code, beta_code, halo,
                               conv_query, conv_key, conv_value)

    kept = lax.dynamic_slice_in_dim(fin, core * half, half, 0)
    away = lax.dynamic_slice_in_dim(fin, (1 - core) * half, half, 0)
    early, both = vmem_call(pair_kernel, [kept.shape] * 2, [], "pair", pos, kept, send(away, 0, 0, 1))
    lines = [row_of(both, z)] + [send(row_of(both, (z + d) % Z_CHIPS), 0, d, 0) for d in range(1, Z_CHIPS)]
    pre, tot = vmem_call(prefix_kernel, [(Z_CHIPS, HD, 2 * HD), (HD, 2 * HD)], [(Z_CHIPS, HD, 2 * HD)],
                         "prefix", pos, *lines)
    tots = [tot] + [send(tot, d, 0, 0) for d in range(1, X_CHIPS)]
    entry, = vmem_call(entry_kernel, [(Z_CHIPS, HD, HD)], [(X_CHIPS, HD, 2 * HD), (X_CHIPS, HD, HD)],
                       "entry", pos, *tots, pre)
    backs = [row_of(entry, z)] + [send(row_of(entry, (z + d) % Z_CHIPS), 0, d, 0) for d in range(1, Z_CHIPS)]
    own, lent = vmem_call(cores_kernel, [(half, HD, HD)] * 2, [(Z_CHIPS, HD, HD)], "cores", pos, *backs, early)
    got = send(lent, 0, 0, 1)

    w_other = [send(w, 0, 0, 1) for w in w_got]

    y = run_out(pos, base, maps, own, got, gate_branch, norm_gain.reshape(1, HD))
    rows = tok_rows // heads
    piece = lambda i: lax.dynamic_slice_in_dim(y, i * rows, rows, 0)
    y_got = [turn(piece((head + d) % heads), d) for d in range(1, heads)]
    total = jnp.dot(piece(head), out_weight, preferred_element_type=F32)
    for yd, wm, wo in zip(y_got, w_got, w_other):
        w = jnp.where(core == 0, cat([wm, wo], 0), cat([wo, wm], 0))
        total = total + jnp.dot(yd, w, preferred_element_type=F32)
    return total.astype(BF16)


def solution(mesh):
    return jax.shard_map(
        shards,
        mesh=mesh,
        in_specs=(P("ctx", "head"),) * 6 + (P(None, "head"),) * 3 + (P(), P("head", None)),
        out_specs=P(("ctx", "head"), None),
        check_vma=False,
    )
```

```python
import functools

import jax, jax.numpy as jnp
from jax import lax
from jax.experimental import pallas as pl
from jax.experimental.pallas import tpu as pltpu
from jax.sharding import PartitionSpec as P

Z_CHIPS, X_CHIPS, CORES = 4, 4, 2

F32, BF16 = jnp.float32, jnp.bfloat16
HD = 128
BLOCK = 64
KERNEL = 4


def split(x):
    hi = x.astype(BF16)
    return hi, (x - hi.astype(F32)).astype(BF16)


def mxu(a, b):
    return jnp.dot(a, b, preferred_element_type=F32)


def cat(parts, axis):
    return jnp.concatenate(parts, axis)


def silu(x):
    return x / (1.0 + jnp.exp(-x))


def pair_rhs(y, left):
    hi, lo = split(y)
    zero = jnp.zeros_like(hi)
    hi = cat([jnp.where(left, hi, zero), jnp.where(left, zero, hi)], 0)
    lo = cat([jnp.where(left, lo, zero), jnp.where(left, zero, lo)], 0)
    row = cat([hi, lo], 1)
    return cat([row, row], 0)


def wide(x):
    return cat(split(x), 1)


def fold(out):
    return out[:, :HD] + out[:, HD:]


def pair_inverses(lows, eye, left, fills):
    raw = [mxu(wide(low), pair_rhs(low, left)) for low in lows]
    fills[0]()
    powers = [fold(r) for r in raw]
    invs = [eye - low for low in lows]
    for fill in fills[1:-1]:
        raw = [mxu(wide(cat([i, p], 0)), pair_rhs(p, left)) for i, p in zip(invs, powers)]
        fill()
        outs = [fold(r) for r in raw]
        invs = [i + o[:BLOCK] for i, o in zip(invs, outs)]
        powers = [o[BLOCK:] for o in outs]
    raw = [mxu(wide(i), pair_rhs(p, left)) for i, p in zip(invs, powers)]
    fills[-1]()
    return [i + fold(r) for i, r in zip(invs, raw)]


def conv(ext, taps):
    acc = None
    for j in range(KERNEL):
        s = KERNEL - 1 - j
        shifted = ext if s == 0 else pltpu.roll(ext, s, 0)
        term = taps[j : j + 1] * shifted[8:]
        acc = term if acc is None else acc + term
    return silu(acc)


def unit(x):
    return x * lax.rsqrt(jnp.sum(x * x, -1, keepdims=True) + 1e-06)


def scan_kernel(pos, q_ref, k_ref, v_ref, gc_ref, bc_ref, halo_ref, cq_ref, ck_ref, cv_ref,
                base_ref, map_ref, kept_ref, away_ref, state, carry, codes):
    n = pl.program_id(0)
    kh = q_ref.shape[1] // HD
    vh = v_ref.shape[1] // HD
    kw, vw = kh * HD, vh * HD

    @pl.when(n == 0)
    def _():
        carry[...] = halo_ref[...].astype(F32)
        codes[0] = jnp.transpose(gc_ref[...].astype(F32))
        codes[1] = jnp.transpose(bc_ref[...].astype(F32))
        r = lax.broadcasted_iota(jnp.int32, (HD, 2 * HD), 0)
        c = lax.broadcasted_iota(jnp.int32, (HD, 2 * HD), 1)
        start = jnp.where(r + HD == c, 1.0, 0.0).astype(F32)
        for h in range(vh):
            state[h] = start

    rows = lax.broadcasted_iota(jnp.int32, (BLOCK, HD), 0)
    lanes = lax.broadcasted_iota(jnp.int32, (BLOCK, HD), 1)
    left = lanes < BLOCK
    cols = jnp.where(left, lanes, lanes - BLOCK)
    causal = rows >= cols
    strict = rows > cols
    eye = jnp.where(rows == cols, 1.0, 0.0).astype(F32)
    left_t = lax.broadcasted_iota(jnp.int32, (HD, HD), 1) < BLOCK

    here = pl.ds(pl.multiple_of(n * BLOCK, BLOCK), BLOCK)
    log_gate = jnp.log1p(-1e-06 * codes[0, here])
    tri = jnp.where(causal, 1.0, 0.0).astype(F32)[:, :BLOCK]
    cum = jnp.dot(tri, log_gate, precision=lax.Precision.HIGHEST, preferred_element_type=F32)
    gamma = jnp.exp(cum)
    beta = codes[1, here] / 1000.0
    beta_g = beta * jnp.exp(-cum)
    last = gamma[BLOCK - 1 :]

    def conved(ref, taps, src, dst, width):
        x = ref[:, src : src + width].astype(F32)
        ext = cat([carry[:, dst : dst + width], x], 0)
        carry[:, dst : dst + width] = x[BLOCK - 8 :]
        return conv(ext, taps[:, src : src + width].astype(F32))

    pairs = range(kh)
    each = range(vh)
    bs = [jnp.broadcast_to(beta[:, h : h + 1], (BLOCK, HD)) for h in each]
    kt2, k2, q2, lows = [], [], [None] * kh, []
    for j in pairs:
        k = unit(conved(k_ref, ck_ref, j * HD, kw + j * HD, HD))
        kt_hi, kt_lo = split(jnp.transpose(cat([k, k], 0)))
        kt2.append((kt_hi, kt_lo))
        k2.append(wide(k))
    for j in pairs:
        row = cat(kt2[j], 1)
        dots = fold(mxu(k2[j], cat([row, row], 0)))
        lows.append(jnp.where(strict, jnp.where(left, bs[2 * j], bs[2 * j + 1]) * dots, 0.0))
    km4, zs, vs = [None] * kh, [None] * vh, [None] * vh

    def fill_q(js):
        for j in js:
            q2[j] = wide(unit(conved(q_ref, cq_ref, j * HD, j * HD, HD)) * HD ** (-0.5))

    def fill_mix(js):
        for j in js:
            row = cat(kt2[j], 1)
            dots = fold(mxu(q2[j], cat([row, row], 0)))
            mh, ml = split(jnp.where(causal, dots, 0.0))
            km = cat([jnp.where(left_t, *kt2[j]), jnp.where(left, mh, ml)], 0)
            km4[j] = cat([km, km], 1)

    def fill_v(hs):
        for h in hs:
            vs[h] = beta_g[:, h : h + 1] * conved(v_ref, cv_ref, h * HD, 2 * kw + h * HD, HD)

    def fill_z(hs):
        for h in hs:
            s_hi, s_lo = split(state[h])
            kq = cat([k2[h // 2], q2[h // 2]], 0)
            zs[h] = mxu(cat([kq, kq[:, :HD]], 1), cat([s_hi, s_hi, s_lo], 0))

    half = vh // 2
    fills = [lambda: fill_q(pairs[: kh // 2]), lambda: fill_q(pairs[kh // 2 :]), lambda: fill_mix(pairs),
             lambda: fill_v(each[:half]), lambda: fill_v(each[half:]), lambda: fill_z(each)]
    invs = pair_inverses(lows, eye, left, fills)
    ts = []
    for inv in invs:
        ih, il = split(inv)
        rh, rl = split(pltpu.roll(inv, BLOCK, 1))
        for t in (jnp.where(left, ih, rl), jnp.where(left, rh, il)):
            ts.append(cat([t, t], 1))
    us = []
    for h in each:
        z = zs[h]
        right = cat([vs[h] - bs[h] * z[:BLOCK, :HD], -bs[h] * z[:BLOCK, HD:]], 1)
        r_hi, r_lo = split(right)
        us.append(mxu(ts[h], cat([r_hi, r_hi, r_lo, r_lo], 0)))
    for h in each:
        u_hi, u_lo = split(us[h])
        ds = mxu(km4[h // 2], cat([u_hi, u_hi, u_lo, u_lo], 0))
        o = gamma[:, h : h + 1] * (zs[h][BLOCK:] + ds[HD:])
        state[h] = last[:, h : h + 1] * (state[h] + ds[:HD])
        base_ref[:, h * HD : (h + 1) * HD] = o[:, :HD]
        o_hi, o_lo = split(o[:, HD:])
        map_ref[:, 2 * h * HD : (2 * h + 1) * HD] = o_hi
        map_ref[:, (2 * h + 1) * HD : (2 * h + 2) * HD] = o_lo

    @pl.when(n == pl.num_programs(0) - 1)
    def _():
        per = vh // 2
        for i in range(per):
            kept_ref[i] = state[pos[2] * per + i]
            away_ref[i] = state[(1 - pos[2]) * per + i]


def run_scan(pos, q, k, v, gc, bc, halo, cq, ck, cv):
    rows = q.shape[0]
    kw, vw = q.shape[1], v.shape[1]
    vh = vw // HD
    row_spec = lambda w: pl.BlockSpec((BLOCK, w), lambda n: (n, 0))
    full = lambda shape: pl.BlockSpec(shape, lambda n: (0,) * len(shape))
    half = (vh // 2, HD, 2 * HD)
    return pl.pallas_call(
        scan_kernel,
        grid=(rows // BLOCK,),
        in_specs=[pl.BlockSpec(memory_space=pltpu.SMEM), row_spec(kw), row_spec(kw), row_spec(vw),
                  full(gc.shape), full(bc.shape), full(halo.shape), full(cq.shape), full(ck.shape), full(cv.shape)],
        out_specs=[row_spec(vw), row_spec(2 * vw), full(half), full(half)],
        out_shape=[jax.ShapeDtypeStruct((rows, vw), F32), jax.ShapeDtypeStruct((rows, 2 * vw), BF16)]
        + [jax.ShapeDtypeStruct(half, F32)] * 2,
        scratch_shapes=[pltpu.VMEM((vh, HD, 2 * HD), F32), pltpu.VMEM((8, 2 * kw + vw), F32),
                        pltpu.VMEM((2, rows, vh), F32)],
        compiler_params=pltpu.CompilerParams(dimension_semantics=("arbitrary",), vmem_limit_bytes=56 << 20),
        name="scan",
    )(pos, q, k, v, gc, bc, halo, cq, ck, cv)


def dot3(a, b):
    a_hi, a_lo = split(a)
    b_hi, b_lo = split(b)
    return mxu(cat([a_hi, a_lo, a_hi], 1), cat([b_hi, b_hi, b_lo], 0))


def then(later, earlier):
    out = dot3(later[:, HD:], earlier)
    return cat([later[:, :HD] + out[:, :HD], out[:, HD:]], 1)


def vmem_call(body, outs, scratch, name, scalars, *arrays):
    return pl.pallas_call(
        body,
        in_specs=[pl.BlockSpec(memory_space=pltpu.SMEM)] + [pl.BlockSpec(memory_space=pltpu.VMEM)] * len(arrays),
        out_specs=[pl.BlockSpec(memory_space=pltpu.VMEM)] * len(outs),
        out_shape=[jax.ShapeDtypeStruct(s, F32) for s in outs],
        scratch_shapes=[pltpu.VMEM(s, F32) for s in scratch],
        name=name,
    )(scalars, *arrays)


def pair_kernel(pos, kept, got, early_ref, o0, o1, o2, o3, both):
    first = pos[2] == 0
    for h in range(Z_CHIPS):
        mine, other = kept[h], got[h]
        early = jnp.where(first, mine, other)
        late = jnp.where(first, other, mine)
        early_ref[h] = early
        both[h] = then(late, early)
    for d, o in enumerate((o0, o1, o2, o3)):
        o[...] = both[(pos[1] + d) % Z_CHIPS]


def prefix_kernel(pos, a0, a1, a2, a3, pre_ref, tot_ref, line):
    z = pos[1]
    for d, a in enumerate((a0, a1, a2, a3)):
        line[(z - d + Z_CHIPS) % Z_CHIPS] = a[...]
    r = lax.broadcasted_iota(jnp.int32, (HD, 2 * HD), 0)
    c = lax.broadcasted_iota(jnp.int32, (HD, 2 * HD), 1)
    pre_ref[0] = jnp.where(r + HD == c, 1.0, 0.0).astype(F32)
    lower = line[0]
    middle = then(line[1], lower)
    pre_ref[1] = lower
    pre_ref[2] = middle
    pre_ref[3] = then(line[2], middle)
    tot_ref[...] = then(then(line[3], line[2]), middle)


def entry_kernel(pos, a0, a1, a2, a3, pre, o0, o1, o2, o3, line, states):
    x, z = pos[0], pos[1]
    for d, a in enumerate((a0, a1, a2, a3)):
        line[(x - d + X_CHIPS) % X_CHIPS] = a[...]
    run = jnp.zeros((HD, HD), F32)
    states[0] = run
    run = line[0, :, :HD]
    states[1] = run
    for i in range(2, X_CHIPS):
        run = line[i - 1, :, :HD] + dot3(line[i - 1, :, HD:], run)
        states[i] = run
    mine = states[x]
    for i in range(Z_CHIPS):
        states[i] = mine if i == 0 else pre[i, :, :HD] + dot3(pre[i, :, HD:], mine)
    for d, o in enumerate((o0, o1, o2, o3)):
        o[...] = states[(z + d) % Z_CHIPS]


def cores_kernel(pos, a0, a1, a2, a3, early, keep_ref, send_ref, line):
    z, first = pos[1], pos[2] == 0
    for d, a in enumerate((a0, a1, a2, a3)):
        line[(z - d + Z_CHIPS) % Z_CHIPS] = a[...]
    for h in range(Z_CHIPS):
        s = line[h]
        t = early[h, :, :HD] + dot3(early[h, :, HD:], s)
        keep_ref[h] = jnp.where(first, s, t)
        send_ref[h] = jnp.where(first, t, s)


def out_kernel(pos, base_ref, map_ref, s_ref, t_ref, gate_ref, gain_ref, o0, o1, o2, o3, rows_ref, *, part):
    h = pl.program_id(0)
    own = pos[2] == part
    row = wide(jnp.where(own, s_ref[h], t_ref[h]))
    o = base_ref[...] + fold(mxu(map_ref[...], cat([row, row], 0)))
    g = gate_ref[...].astype(F32)
    y = o * lax.rsqrt(jnp.mean(o * o, -1, keepdims=True) + 1e-06) * gain_ref[...] * silu(g)
    rows_ref[...] = y
    size = o0.shape[0]
    for d, ref in enumerate((o0, o1, o2, o3)):
        start = pl.multiple_of((pos[3] + d) % 4 * size, size)
        ref[...] = rows_ref[pl.ds(start, size), :].astype(BF16)


def run_out(pos, base, maps, kept, got, gate, gain, part):
    rows = base.shape[0]
    per = kept.shape[0]
    col = lambda w: pl.BlockSpec((rows, w), lambda h: (0, h + part * per))
    full = lambda a: pl.BlockSpec(a.shape, lambda h: (0,) * a.ndim)
    return pl.pallas_call(
        functools.partial(out_kernel, part=part),
        grid=(per,),
        in_specs=[pl.BlockSpec(memory_space=pltpu.SMEM), col(HD), col(2 * HD), full(kept), full(got), col(HD), full(gain)],
        out_specs=[pl.BlockSpec((rows // 4, HD), lambda h: (0, h))] * 4,
        out_shape=[jax.ShapeDtypeStruct((rows // 4, per * HD), BF16)] * 4,
        scratch_shapes=[pltpu.VMEM((rows, HD), F32)],
        name="out" + str(part),
    )(pos, base, maps, kept, got, gate, gain)


def project_kernel(pos, *refs, part, owns, pieces, extra):
    refs = list(refs)
    y_own = [refs.pop(0) for _ in owns]
    w_own = [refs.pop(0) for _ in owns]
    y_got = [refs.pop(0) for _ in range(pieces)]
    w_here = [refs.pop(0) for _ in range(pieces)]
    w_there = [refs.pop(0) for _ in range(pieces)]
    total = [refs.pop(0)[...]] if extra else []
    out_ref, acc = refs
    for y, w in zip(y_own, w_own):
        total.append(mxu(y[...], w[...]))
    if total:
        acc[...] = sum(total[1:], total[0])

    def gather(ws):
        out = acc[...]
        for y, w in zip(y_got, ws):
            out = out + mxu(y[...], w[...])
        out_ref[...] = out.astype(out_ref.dtype)

    @pl.when(pos[2] == part)
    def _():
        gather(w_here)

    @pl.when(pos[2] != part)
    def _():
        gather(w_there)


def project(pos, part, owns, y_own, weight, y_got, w_here, w_there, acc, dtype, tile=512):
    rows, depth = y_got[0].shape
    width = weight.shape[1]
    tiled = lambda f: pl.BlockSpec((depth, tile), f)
    whole = lambda a: pl.BlockSpec(a.shape, lambda n, pos: (0, 0))
    piece = pl.BlockSpec((rows, tile), lambda n, pos: (0, n))
    here = tiled(lambda n, pos: (0, jnp.where(pos[2] == part, n, 0)))
    there = tiled(lambda n, pos: (0, jnp.where(pos[2] == part, 0, n)))
    own_specs = [pl.BlockSpec((depth, tile), functools.partial(lambda i, n, pos: (i, n), i)) for i in owns]
    body = functools.partial(project_kernel, part=part, owns=owns, pieces=len(y_got), extra=acc is not None)
    return pl.pallas_call(
        body,
        grid_spec=pltpu.PrefetchScalarGridSpec(
            num_scalar_prefetch=1,
            grid=(width // tile,),
            in_specs=[whole(y) for y in y_own] + own_specs + [whole(y) for y in y_got]
            + [here] * len(w_here) + [there] * len(w_there) + [piece] * (acc is not None),
            out_specs=piece,
            scratch_shapes=[pltpu.VMEM((rows, tile), F32)],
        ),
        out_shape=jax.ShapeDtypeStruct((rows, width), dtype),
        name="project" + str(part),
    )(pos, *y_own, *([weight] * len(owns)), *y_got, *w_here, *w_there, *([] if acc is None else [acc]))


def ctx_route(dx, dz, dc):
    def dest(i):
        x, z, c = i // (Z_CHIPS * CORES), (i // CORES) % Z_CHIPS, i % CORES
        return ((x + dx) % X_CHIPS * Z_CHIPS + (z + dz) % Z_CHIPS) * CORES + (c + dc) % CORES
    return [(i, dest(i)) for i in range(X_CHIPS * Z_CHIPS * CORES)]


def shards(query_raw, key_raw, value_raw, gate_branch, gate_code, beta_code,
           conv_query, conv_key, conv_value, norm_gain, out_weight):
    tok_rows = query_raw.shape[0]
    ctx = lax.axis_index("ctx")
    head = lax.axis_index("head")
    heads = lax.axis_size("head")
    x, z, core = ctx // (Z_CHIPS * CORES), (ctx // CORES) % Z_CHIPS, ctx % CORES
    pos = jnp.stack([x, z, core, head]).astype(jnp.int32)
    send = lambda a, dx, dz, dc: lax.ppermute(a, "ctx", ctx_route(dx, dz, dc))
    turn = lambda a, d: lax.ppermute(a, "head", [(i, (i + d) % heads) for i in range(heads)])
    hops = (1, 3, 2)
    barrier = lax.optimization_barrier

    rim = cat([a[tok_rows - 8 :] for a in (query_raw, key_raw, value_raw)], 1)
    halo = lax.ppermute(rim, "ctx", [(i, i + 1) for i in range(lax.axis_size("ctx") - 1)])

    w_rows = out_weight.shape[0] // CORES
    w_mine = lax.dynamic_slice_in_dim(out_weight, core * w_rows, w_rows, 0)
    w_got = [turn(w_mine, d) for d in hops]

    base, maps, kept, away = run_scan(pos, query_raw, key_raw, value_raw, gate_code.T, beta_code.T, halo,
                                      conv_query, conv_key, conv_value)

    line, full = (HD, 2 * HD), (Z_CHIPS, HD, 2 * HD)
    early, *both = vmem_call(pair_kernel, [full] + [line] * 4, [full], "pair", pos, kept, send(away, 0, 0, 1))
    lines = [both[0]] + [send(both[d], 0, d, 0) for d in range(1, Z_CHIPS)]
    pre, tot = vmem_call(prefix_kernel, [full, line], [full], "prefix", pos, *lines)
    tots = [tot] + [send(tot, d, 0, 0) for d in range(1, X_CHIPS)]
    entry = vmem_call(entry_kernel, [(HD, HD)] * 4, [full, (Z_CHIPS, HD, HD)], "entry", pos, *tots, pre)
    backs = [entry[0]] + [send(entry[d], 0, d, 0) for d in range(1, Z_CHIPS)]
    own, lent = vmem_call(cores_kernel, [(Z_CHIPS, HD, HD)] * 2, [(Z_CHIPS, HD, HD)], "cores", pos, *backs, early)
    got = send(lent, 0, 0, 1)

    gain = norm_gain.reshape(1, HD)
    got, w_late = barrier((got, w_got))
    y_a = run_out(pos, base, maps, own, got, gate_branch, gain, 0)
    w_other = [send(w, 0, 0, 1) for w in w_late]
    a_got = [turn(y_a[d], d) for d in hops]
    y_b = run_out(pos, base, maps, own, got, gate_branch, gain, 1)
    b_got = [turn(y_b[d], d) for d in hops]
    acc = project(pos, 0, (0, 1), [y_a[0], y_b[0]], out_weight, a_got, w_late, w_other, None, F32)
    return project(pos, 1, (), [], out_weight, b_got, w_late, w_other, acc, BF16)


def solution(mesh):
    return jax.shard_map(
        shards,
        mesh=mesh,
        in_specs=(P("ctx", "head"),) * 6 + (P(None, "head"),) * 3 + (P(), P("head", None)),
        out_specs=P(("ctx", "head"), None),
        check_vma=False,
    )
```

```python
import functools

import jax, jax.numpy as jnp
from jax import lax
from jax.experimental import pallas as pl
from jax.experimental.pallas import tpu as pltpu
from jax.sharding import PartitionSpec as P


Z_CHIPS, X_CHIPS, CORES = 4, 4, 2

F32, BF16 = jnp.float32, jnp.bfloat16
HD = 128
BLOCK = 64
KERNEL = 4
LIMIT = 12 << 20


def split(x):
    hi = x.astype(BF16)
    return hi, (x - hi.astype(F32)).astype(BF16)


def mxu(a, b):
    return jnp.dot(a, b, preferred_element_type=F32)


def cat(parts, axis):
    return jnp.concatenate(parts, axis)


def silu(x):
    return x / (1.0 + jnp.exp(-x))


def pair_rhs(y, left):
    hi, lo = split(y)
    zero = jnp.zeros_like(hi)
    hi = cat([jnp.where(left, hi, zero), jnp.where(left, zero, hi)], 0)
    lo = cat([jnp.where(left, lo, zero), jnp.where(left, zero, lo)], 0)
    row = cat([hi, lo], 1)
    return cat([row, row], 0)


def wide(x):
    return cat(split(x), 1)


def fold(out):
    return out[:, :HD] + out[:, HD:]


def pair_inverses(lows, eye, left, fills):
    raw = [mxu(wide(low), pair_rhs(low, left)) for low in lows]
    fills[0]()
    powers = [fold(r) for r in raw]
    invs = [eye - low for low in lows]
    for fill in fills[1:-1]:
        raw = [mxu(wide(cat([i, p], 0)), pair_rhs(p, left)) for i, p in zip(invs, powers)]
        fill()
        outs = [fold(r) for r in raw]
        invs = [i + o[:BLOCK] for i, o in zip(invs, outs)]
        powers = [o[BLOCK:] for o in outs]
    raw = [mxu(wide(i), pair_rhs(p, left)) for i, p in zip(invs, powers)]
    fills[-1]()
    return [i + fold(r) for i, r in zip(invs, raw)]


def conv(ext, taps):
    acc = None
    for j in range(KERNEL):
        s = KERNEL - 1 - j
        shifted = ext if s == 0 else pltpu.roll(ext, s, 0)
        term = taps[j : j + 1] * shifted[8:]
        acc = term if acc is None else acc + term
    return silu(acc)


def unit(x):
    return x * lax.rsqrt(jnp.sum(x * x, -1, keepdims=True) + 1e-06)


def scan_kernel(pos, q_ref, k_ref, v_ref, gc_ref, bc_ref, halo_ref, cq_ref, ck_ref, cv_ref,
                base_ref, map_ref, kept_ref, away_ref, state, carry, codes):
    n = pl.program_id(0)
    kh = q_ref.shape[1] // HD
    vh = v_ref.shape[1] // HD
    kw = kh * HD

    @pl.when(n == 0)
    def _():
        carry[...] = halo_ref[...].astype(F32)
        codes[0] = jnp.transpose(gc_ref[...].astype(F32))
        codes[1] = jnp.transpose(bc_ref[...].astype(F32))
        r = lax.broadcasted_iota(jnp.int32, (HD, 2 * HD), 0)
        c = lax.broadcasted_iota(jnp.int32, (HD, 2 * HD), 1)
        start = jnp.where(r + HD == c, 1.0, 0.0).astype(F32)
        for h in range(vh):
            state[h] = start

    rows = lax.broadcasted_iota(jnp.int32, (BLOCK, HD), 0)
    lanes = lax.broadcasted_iota(jnp.int32, (BLOCK, HD), 1)
    left = lanes < BLOCK
    cols = jnp.where(left, lanes, lanes - BLOCK)
    causal = rows >= cols
    strict = rows > cols
    eye = jnp.where(rows == cols, 1.0, 0.0).astype(F32)
    left_t = lax.broadcasted_iota(jnp.int32, (HD, HD), 1) < BLOCK

    here = pl.ds(pl.multiple_of(n * BLOCK, BLOCK), BLOCK)
    log_gate = jnp.log1p(-1e-06 * codes[0, here])
    tri = jnp.where(causal, 1.0, 0.0).astype(F32)[:, :BLOCK]
    cum = jnp.dot(tri, log_gate, precision=lax.Precision.HIGHEST, preferred_element_type=F32)
    gamma = jnp.exp(cum)
    beta = codes[1, here] / 1000.0
    beta_g = beta * jnp.exp(-cum)
    last = gamma[BLOCK - 1 :]

    def conved(ref, taps, src, dst, width):
        x = ref[:, src : src + width].astype(F32)
        ext = cat([carry[:, dst : dst + width], x], 0)
        carry[:, dst : dst + width] = x[BLOCK - 8 :]
        return conv(ext, taps[:, src : src + width].astype(F32))

    pairs = range(kh)
    each = range(vh)
    bs = [jnp.broadcast_to(beta[:, h : h + 1], (BLOCK, HD)) for h in each]
    kt2, k2, q2, lows = [], [], [None] * kh, []
    for j in pairs:
        k = unit(conved(k_ref, ck_ref, j * HD, kw + j * HD, HD))
        kt_hi, kt_lo = split(jnp.transpose(cat([k, k], 0)))
        kt2.append((kt_hi, kt_lo))
        k2.append(wide(k))
    for j in pairs:
        row = cat(kt2[j], 1)
        dots = fold(mxu(k2[j], cat([row, row], 0)))
        lows.append(jnp.where(strict, jnp.where(left, bs[2 * j], bs[2 * j + 1]) * dots, 0.0))
    km4, zs, vs = [None] * kh, [None] * vh, [None] * vh

    def fill_q(js):
        for j in js:
            q2[j] = wide(unit(conved(q_ref, cq_ref, j * HD, j * HD, HD)) * HD ** (-0.5))

    def fill_mix(js):
        for j in js:
            row = cat(kt2[j], 1)
            dots = fold(mxu(q2[j], cat([row, row], 0)))
            mh, ml = split(jnp.where(causal, dots, 0.0))
            km = cat([jnp.where(left_t, *kt2[j]), jnp.where(left, mh, ml)], 0)
            km4[j] = cat([km, km], 1)

    def fill_v(hs):
        for h in hs:
            vs[h] = beta_g[:, h : h + 1] * conved(v_ref, cv_ref, h * HD, 2 * kw + h * HD, HD)

    def fill_z(hs):
        for h in hs:
            s_hi, s_lo = split(state[h])
            kq = cat([k2[h // 2], q2[h // 2]], 0)
            zs[h] = mxu(cat([kq, kq[:, :HD]], 1), cat([s_hi, s_hi, s_lo], 0))

    half = vh // 2
    fills = [lambda: fill_q(pairs[: kh // 2]), lambda: fill_q(pairs[kh // 2 :]), lambda: fill_mix(pairs),
             lambda: fill_v(each[:half]), lambda: fill_v(each[half:]), lambda: fill_z(each)]
    invs = pair_inverses(lows, eye, left, fills)
    ts = []
    for inv in invs:
        ih, il = split(inv)
        rh, rl = split(pltpu.roll(inv, BLOCK, 1))
        for t in (jnp.where(left, ih, rl), jnp.where(left, rh, il)):
            ts.append(cat([t, t], 1))
    us = []
    for h in each:
        z = zs[h]
        right = cat([vs[h] - bs[h] * z[:BLOCK, :HD], -bs[h] * z[:BLOCK, HD:]], 1)
        r_hi, r_lo = split(right)
        us.append(mxu(ts[h], cat([r_hi, r_hi, r_lo, r_lo], 0)))
    for h in each:
        u_hi, u_lo = split(us[h])
        ds = mxu(km4[h // 2], cat([u_hi, u_hi, u_lo, u_lo], 0))
        o = gamma[:, h : h + 1] * (zs[h][BLOCK:] + ds[HD:])
        state[h] = last[:, h : h + 1] * (state[h] + ds[:HD])
        base_ref[here, h * HD : (h + 1) * HD] = o[:, :HD]
        o_hi, o_lo = split(o[:, HD:])
        map_ref[here, 2 * h * HD : (2 * h + 1) * HD] = o_hi
        map_ref[here, (2 * h + 1) * HD : (2 * h + 2) * HD] = o_lo

    @pl.when(n == pl.num_programs(0) - 1)
    def _():
        per = vh // 2
        for i in range(per):
            kept_ref[i] = state[pos[2] * per + i]
            away_ref[i] = state[(1 - pos[2]) * per + i]


def run_scan(pos, q, k, v, gc, bc, halo, cq, ck, cv):
    rows = q.shape[0]
    kw, vw = q.shape[1], v.shape[1]
    vh = vw // HD
    row_spec = lambda w: pl.BlockSpec((BLOCK, w), lambda n: (n, 0))
    full = lambda shape: pl.BlockSpec(shape, lambda n: (0,) * len(shape))
    half = (vh // 2, HD, 2 * HD)
    return pl.pallas_call(
        scan_kernel,
        grid=(rows // BLOCK,),
        in_specs=[pl.BlockSpec(memory_space=pltpu.SMEM), row_spec(kw), row_spec(kw), row_spec(vw),
                  full(gc.shape), full(bc.shape), full(halo.shape), full(cq.shape), full(ck.shape), full(cv.shape)],
        out_specs=[pl.BlockSpec(memory_space=pltpu.VMEM)] * 4,
        out_shape=[jax.ShapeDtypeStruct((rows, vw), F32), jax.ShapeDtypeStruct((rows, 2 * vw), BF16)]
        + [jax.ShapeDtypeStruct(half, F32)] * 2,
        scratch_shapes=[pltpu.VMEM((vh, HD, 2 * HD), F32), pltpu.VMEM((8, 2 * kw + vw), F32),
                        pltpu.VMEM((2, rows, vh), F32)],
        compiler_params=pltpu.CompilerParams(dimension_semantics=("arbitrary",), vmem_limit_bytes=20 << 20),
        name="scan",
    )(pos, q, k, v, gc, bc, halo, cq, ck, cv)


def dot3(a, b):
    a_hi, a_lo = split(a)
    b_hi, b_lo = split(b)
    return mxu(cat([a_hi, a_lo, a_hi], 1), cat([b_hi, b_hi, b_lo], 0))


def then(later, earlier):
    out = dot3(later[:, HD:], earlier)
    return cat([later[:, :HD] + out[:, :HD], out[:, HD:]], 1)


def vmem_call(body, outs, scratch, scalars, *arrays):
    return pl.pallas_call(
        body,
        in_specs=[pl.BlockSpec(memory_space=pltpu.SMEM)] + [pl.BlockSpec(memory_space=pltpu.VMEM)] * len(arrays),
        out_specs=[pl.BlockSpec(memory_space=pltpu.VMEM)] * len(outs),
        out_shape=[jax.ShapeDtypeStruct(s, F32) for s in outs],
        scratch_shapes=[pltpu.VMEM(s, F32) for s in scratch],
        compiler_params=pltpu.CompilerParams(vmem_limit_bytes=LIMIT),
    )(scalars, *arrays)


def pair_kernel(pos, kept, got, early_ref, o0, o1, o2, o3, both):
    first = pos[2] == 0
    for h in range(Z_CHIPS):
        mine, other = kept[h], got[h]
        early = jnp.where(first, mine, other)
        late = jnp.where(first, other, mine)
        early_ref[h] = early
        both[h] = then(late, early)
    for d, o in enumerate((o0, o1, o2, o3)):
        o[...] = both[(pos[1] + d) % Z_CHIPS]


def prefix_kernel(pos, a0, a1, a2, a3, pre_ref, tot_ref, line):
    z = pos[1]
    for d, a in enumerate((a0, a1, a2, a3)):
        line[(z - d + Z_CHIPS) % Z_CHIPS] = a[...]
    r = lax.broadcasted_iota(jnp.int32, (HD, 2 * HD), 0)
    c = lax.broadcasted_iota(jnp.int32, (HD, 2 * HD), 1)
    pre_ref[0] = jnp.where(r + HD == c, 1.0, 0.0).astype(F32)
    lower = line[0]
    middle = then(line[1], lower)
    pre_ref[1] = lower
    pre_ref[2] = middle
    pre_ref[3] = then(line[2], middle)
    tot_ref[...] = then(then(line[3], line[2]), middle)


def entry_kernel(pos, a0, a1, a2, a3, pre, o0, o1, o2, o3, line, states):
    x, z = pos[0], pos[1]
    for d, a in enumerate((a0, a1, a2, a3)):
        line[(x - d + X_CHIPS) % X_CHIPS] = a[...]
    run = jnp.zeros((HD, HD), F32)
    states[0] = run
    run = line[0, :, :HD]
    states[1] = run
    for i in range(2, X_CHIPS):
        run = line[i - 1, :, :HD] + dot3(line[i - 1, :, HD:], run)
        states[i] = run
    mine = states[x]
    for i in range(Z_CHIPS):
        states[i] = mine if i == 0 else pre[i, :, :HD] + dot3(pre[i, :, HD:], mine)
    for d, o in enumerate((o0, o1, o2, o3)):
        o[...] = states[(z + d) % Z_CHIPS]


def cores_kernel(pos, a0, a1, a2, a3, early, keep_ref, send_ref, line):
    z, first = pos[1], pos[2] == 0
    for d, a in enumerate((a0, a1, a2, a3)):
        line[(z - d + Z_CHIPS) % Z_CHIPS] = a[...]
    for h in range(Z_CHIPS):
        s = line[h]
        t = early[h, :, :HD] + dot3(early[h, :, HD:], s)
        keep_ref[h] = jnp.where(first, s, t)
        send_ref[h] = jnp.where(first, t, s)


def out_kernel(pos, base_ref, map_ref, s_ref, t_ref, gate_ref, gain_ref, o0, o1, o2, o3, rights, *, part):
    per = s_ref.shape[0]
    own = pos[2] == part
    for h in range(per):
        row = wide(jnp.where(own, s_ref[h], t_ref[h]))
        rights[h] = cat([row, row], 0)
    size = o0.shape[0]
    gain = gain_ref[...]
    for d, ref in enumerate((o0, o1, o2, o3)):
        rows = pl.ds(pl.multiple_of((pos[3] + d) % 4 * size, size), size)

        def step(h, _):
            at = (part * per + h) * HD
            cols = pl.ds(pl.multiple_of(at, HD), HD)
            o = base_ref[rows, cols] + fold(mxu(map_ref[rows, pl.ds(pl.multiple_of(2 * at, HD), 2 * HD)], rights[h]))
            g = gate_ref[rows, cols].astype(F32)
            y = o * lax.rsqrt(jnp.mean(o * o, -1, keepdims=True) + 1e-06) * gain * silu(g)
            ref[:, pl.ds(pl.multiple_of(h * HD, HD), HD)] = y.astype(BF16)
            return 0

        lax.fori_loop(0, per, step, 0)


def run_out(pos, base, maps, kept, got, gate, gain, part):
    rows = base.shape[0]
    per = kept.shape[0]
    vmem = pl.BlockSpec(memory_space=pltpu.VMEM)
    return pl.pallas_call(
        functools.partial(out_kernel, part=part),
        in_specs=[pl.BlockSpec(memory_space=pltpu.SMEM)] + [vmem] * 6,
        out_specs=[vmem] * 4,
        out_shape=[jax.ShapeDtypeStruct((rows // 4, per * HD), BF16)] * 4,
        scratch_shapes=[pltpu.VMEM((per, 2 * HD, 2 * HD), BF16)],
        compiler_params=pltpu.CompilerParams(vmem_limit_bytes=LIMIT),
    )(pos, base, maps, kept, got, gate, gain)


def project_kernel(pos, *refs, part, count, offset, extra, final):
    ys, here, there = refs[:count], refs[count : 2 * count], refs[2 * count : 3 * count]
    acc_ref = refs[3 * count] if extra else None
    out_ref, *more = refs[3 * count + extra :]
    depth = ys[0].shape[1]
    tile = 512
    tiles = out_ref.shape[1] // tile

    def sweep(ws):
        for t in range(tiles):
            cols = slice(t * tile, (t + 1) * tile)
            total = acc_ref[:, cols] if extra else None
            for p in range(count):
                term = mxu(ys[p][...], ws[p][offset * p : offset * p + depth, cols])
                total = term if total is None else total + term
            if final:
                more[0][t] = total.astype(BF16)
                store(t).start()
            else:
                out_ref[:, cols] = total

    def store(t):
        return pltpu.make_async_copy(more[0].at[t], out_ref.at[:, pl.ds(t * tile, tile)], more[1].at[t])

    if offset:
        sweep(here)
    else:
        pl.when(pos[2] == part)(lambda: sweep(here))
        pl.when(pos[2] != part)(lambda: sweep(there))
    if final:
        for t in range(tiles):
            store(t).wait()


def project(pos, part, ys, here, there, offset, acc, dtype):
    rows, _ = ys[0].shape
    width = here[0].shape[1]
    count = len(ys)
    final = dtype == BF16
    vmem, hbm = pl.BlockSpec(memory_space=pltpu.VMEM), pl.BlockSpec(memory_space=pl.ANY)
    accs = [] if acc is None else [acc]
    return pl.pallas_call(
        functools.partial(project_kernel, part=part, count=count, offset=offset, extra=len(accs), final=final),
        in_specs=[pl.BlockSpec(memory_space=pltpu.SMEM)] + [vmem] * (3 * count + len(accs)),
        out_specs=hbm if final else vmem,
        out_shape=jax.ShapeDtypeStruct((rows, width), dtype),
        scratch_shapes=[pltpu.VMEM((width // 512, rows, 512), dtype), pltpu.SemaphoreType.DMA((width // 512,))] * final,
        compiler_params=pltpu.CompilerParams(vmem_limit_bytes=LIMIT),
    )(pos, *ys, *here, *there, *accs)


def rim_kernel(q, k, v, out_ref, sem):
    copies, at = [], 0
    for i, ref in enumerate((q, k, v)):
        rows, width = ref.shape
        copies.append(pltpu.make_async_copy(ref.at[pl.ds(rows - 8, 8)], out_ref.at[:, pl.ds(at, width)], sem.at[i]))
        at += width
    for c in copies:
        c.start()
    for c in copies:
        c.wait()


def run_rim(q, k, v):
    hbm = pl.BlockSpec(memory_space=pl.ANY)
    return pl.pallas_call(
        rim_kernel,
        in_specs=[hbm] * 3,
        out_specs=pl.BlockSpec(memory_space=pltpu.VMEM),
        out_shape=jax.ShapeDtypeStruct((8, q.shape[1] + k.shape[1] + v.shape[1]), BF16),
        scratch_shapes=[pltpu.SemaphoreType.DMA((3,))],
        name="rim",
    )(q, k, v)


def half_kernel(pos, w, out_ref, sem):
    rows = out_ref.shape[0]
    start = pl.multiple_of(pos[2] * rows, rows)
    copy = pltpu.make_async_copy(w.at[pl.ds(start, rows)], out_ref, sem)
    copy.start()
    copy.wait()


def run_half(pos, weight, rows):
    return pl.pallas_call(
        half_kernel,
        in_specs=[pl.BlockSpec(memory_space=pltpu.SMEM), pl.BlockSpec(memory_space=pl.ANY)],
        out_specs=pl.BlockSpec(memory_space=pltpu.VMEM),
        out_shape=jax.ShapeDtypeStruct((rows, weight.shape[1]), BF16),
        scratch_shapes=[pltpu.SemaphoreType.DMA(())],
        name="half",
    )(pos, weight)


def ctx_route(dx, dz, dc):
    def dest(i):
        x, z, c = i // (Z_CHIPS * CORES), (i // CORES) % Z_CHIPS, i % CORES
        return ((x + dx) % X_CHIPS * Z_CHIPS + (z + dz) % Z_CHIPS) * CORES + (c + dc) % CORES

    return [(i, dest(i)) for i in range(X_CHIPS * Z_CHIPS * CORES)]


def shards(query_raw, key_raw, value_raw, gate_branch, gate_code, beta_code,
           conv_query, conv_key, conv_value, norm_gain, out_weight):
    ctx = lax.axis_index("ctx")
    head = lax.axis_index("head")
    heads = lax.axis_size("head")
    x, z, core = ctx // (Z_CHIPS * CORES), (ctx // CORES) % Z_CHIPS, ctx % CORES
    pos = jnp.stack([x, z, core, head]).astype(jnp.int32)
    send = lambda a, dx, dz, dc: lax.ppermute(a, "ctx", ctx_route(dx, dz, dc))
    turn = lambda a, d: lax.ppermute(a, "head", [(i, (i + d) % heads) for i in range(heads)])
    hops = (1, 3, 2)
    barrier = lax.optimization_barrier

    n_ctx = lax.axis_size("ctx")
    raws = [pltpu.with_memory_space_constraint(a, pltpu.HBM) for a in (query_raw, key_raw, value_raw)]
    w_rows = out_weight.shape[0] // CORES
    halo = lax.ppermute(run_rim(*raws), "ctx", [(i, i + 1) for i in range(n_ctx - 1)])
    w_mine = run_half(pos, out_weight, w_rows)
    w_got = [turn(w_mine, d) for d in hops]

    base, maps, kept, away = run_scan(pos, *raws, gate_code.T, beta_code.T, halo,
                                      conv_query, conv_key, conv_value)

    line, full = (HD, 2 * HD), (Z_CHIPS, HD, 2 * HD)
    early, *both = vmem_call(pair_kernel, [full] + [line] * 4, [full], pos, kept, send(away, 0, 0, 1))
    lines = [both[0]] + [send(both[d], 0, d, 0) for d in range(1, Z_CHIPS)]
    pre, tot = vmem_call(prefix_kernel, [full, line], [full], pos, *lines)
    tots = [tot] + [send(tot, d, 0, 0) for d in range(1, X_CHIPS)]
    entry = vmem_call(entry_kernel, [(HD, HD)] * 4, [full, (Z_CHIPS, HD, HD)], pos, *tots, pre)
    backs = [entry[0]] + [send(entry[d], 0, d, 0) for d in range(1, Z_CHIPS)]
    own, lent = vmem_call(cores_kernel, [(Z_CHIPS, HD, HD)] * 2, [(Z_CHIPS, HD, HD)], pos, *backs, early)
    got = send(lent, 0, 0, 1)

    gain = norm_gain.reshape(1, HD)
    y_a = run_out(pos, base, maps, own, got, gate_branch, gain, 0)
    a_got = [turn(y_a[d], d) for d in hops]
    _, w_late = barrier((y_a[0], w_got))
    w_other = [send(w, 0, 0, 1) for w in w_late]
    y_b = run_out(pos, base, maps, own, got, gate_branch, gain, 1)
    b_got = [turn(y_b[d], d) for d in hops]
    acc = project(pos, 0, [y_a[0], y_b[0]], [out_weight] * 2, [out_weight] * 2, w_rows, None, F32)
    acc = project(pos, 0, a_got, w_late, w_other, 0, acc, F32)
    return project(pos, 1, b_got, w_late, w_other, 0, acc, BF16)


def solution(mesh):
    return jax.shard_map(
        shards,
        mesh=mesh,
        in_specs=(P("ctx", "head"),) * 6 + (P(None, "head"),) * 3 + (P(), P("head", None)),
        out_specs=P(("ctx", "head"), None),
        check_vma=False,
    )
```

```python
import functools

import jax, jax.numpy as jnp
from jax import lax
from jax.experimental import pallas as pl
from jax.experimental.pallas import tpu as pltpu
from jax.sharding import PartitionSpec as P


Z_CHIPS, X_CHIPS, CORES = 4, 4, 2

F32, BF16 = jnp.float32, jnp.bfloat16
HD = 128
BLOCK = 64
KERNEL = 4
LIMIT = 6 << 20


def split(x):
    hi = x.astype(BF16)
    return hi, (x - hi.astype(F32)).astype(BF16)


def mxu(a, b):
    return jnp.dot(a, b, preferred_element_type=F32)


def cat(parts, axis):
    return jnp.concatenate(parts, axis)


def silu(x):
    return x / (1.0 + jnp.exp(-x))


def pair_rhs(y, left):
    hi, lo = split(y)
    zero = jnp.zeros_like(hi)
    hi = cat([jnp.where(left, hi, zero), jnp.where(left, zero, hi)], 0)
    lo = cat([jnp.where(left, lo, zero), jnp.where(left, zero, lo)], 0)
    row = cat([hi, lo], 1)
    return cat([row, row], 0)


def wide(x):
    return cat(split(x), 1)


def fold(out):
    return out[:, :HD] + out[:, HD:]


def pair_inverses(lows, eye, left, fills):
    raw = [mxu(wide(low), pair_rhs(low, left)) for low in lows]
    fills[0]()
    powers = [fold(r) for r in raw]
    invs = [eye - low for low in lows]
    for fill in fills[1:-1]:
        raw = [mxu(wide(cat([i, p], 0)), pair_rhs(p, left)) for i, p in zip(invs, powers)]
        fill()
        outs = [fold(r) for r in raw]
        invs = [i + o[:BLOCK] for i, o in zip(invs, outs)]
        powers = [o[BLOCK:] for o in outs]
    raw = [mxu(wide(i), pair_rhs(p, left)) for i, p in zip(invs, powers)]
    fills[-1]()
    return [i + fold(r) for i, r in zip(invs, raw)]


def conv(ext, taps):
    acc = None
    for j in range(KERNEL):
        s = KERNEL - 1 - j
        shifted = ext if s == 0 else pltpu.roll(ext, s, 0)
        term = taps[j : j + 1] * shifted[8:]
        acc = term if acc is None else acc + term
    return silu(acc)


def unit(x):
    return x * lax.rsqrt(jnp.sum(x * x, -1, keepdims=True) + 1e-06)


def scan_kernel(pos, q_ref, k_ref, v_ref, gc_ref, bc_ref, halo_ref, cq_ref, ck_ref, cv_ref,
                base_ref, map_ref, kept_ref, away_ref, state, carry, codes):
    n = pl.program_id(0)
    kh = q_ref.shape[1] // HD
    vh = v_ref.shape[1] // HD
    kw = kh * HD

    @pl.when(n == 0)
    def _():
        carry[...] = halo_ref[...].astype(F32)
        codes[0] = jnp.transpose(gc_ref[...].astype(F32))
        codes[1] = jnp.transpose(bc_ref[...].astype(F32))
        r = lax.broadcasted_iota(jnp.int32, (HD, 2 * HD), 0)
        c = lax.broadcasted_iota(jnp.int32, (HD, 2 * HD), 1)
        start = jnp.where(r + HD == c, 1.0, 0.0).astype(F32)
        for h in range(vh):
            state[h] = start

    rows = lax.broadcasted_iota(jnp.int32, (BLOCK, HD), 0)
    lanes = lax.broadcasted_iota(jnp.int32, (BLOCK, HD), 1)
    left = lanes < BLOCK
    cols = jnp.where(left, lanes, lanes - BLOCK)
    causal = rows >= cols
    strict = rows > cols
    eye = jnp.where(rows == cols, 1.0, 0.0).astype(F32)
    left_t = lax.broadcasted_iota(jnp.int32, (HD, HD), 1) < BLOCK

    here = pl.ds(pl.multiple_of(n * BLOCK, BLOCK), BLOCK)
    log_gate = jnp.log1p(-1e-06 * codes[0, here])
    tri = jnp.where(causal, 1.0, 0.0).astype(F32)[:, :BLOCK]
    cum = jnp.dot(tri, log_gate, precision=lax.Precision.HIGHEST, preferred_element_type=F32)
    gamma = jnp.exp(cum)
    beta = codes[1, here] / 1000.0
    beta_g = beta * jnp.exp(-cum)
    last = gamma[BLOCK - 1 :]

    def conved(ref, taps, src, dst, width):
        x = ref[:, src : src + width].astype(F32)
        ext = cat([carry[:, dst : dst + width], x], 0)
        carry[:, dst : dst + width] = x[BLOCK - 8 :]
        return conv(ext, taps[:, src : src + width].astype(F32))

    pairs = range(kh)
    each = range(vh)
    bs = [jnp.broadcast_to(beta[:, h : h + 1], (BLOCK, HD)) for h in each]
    kt2, k2, q2, lows = [], [], [None] * kh, []
    for j in pairs:
        k = unit(conved(k_ref, ck_ref, j * HD, kw + j * HD, HD))
        kt_hi, kt_lo = split(jnp.transpose(cat([k, k], 0)))
        kt2.append((kt_hi, kt_lo))
        k2.append(wide(k))
    for j in pairs:
        row = cat(kt2[j], 1)
        dots = fold(mxu(k2[j], cat([row, row], 0)))
        lows.append(jnp.where(strict, jnp.where(left, bs[2 * j], bs[2 * j + 1]) * dots, 0.0))
    km4, zs, vs = [None] * kh, [None] * vh, [None] * vh

    def fill_q(js):
        for j in js:
            q2[j] = wide(unit(conved(q_ref, cq_ref, j * HD, j * HD, HD)) * HD ** (-0.5))

    def fill_mix(js):
        for j in js:
            row = cat(kt2[j], 1)
            dots = fold(mxu(q2[j], cat([row, row], 0)))
            mh, ml = split(jnp.where(causal, dots, 0.0))
            km = cat([jnp.where(left_t, *kt2[j]), jnp.where(left, mh, ml)], 0)
            km4[j] = cat([km, km], 1)

    def fill_v(hs):
        for h in hs:
            vs[h] = beta_g[:, h : h + 1] * conved(v_ref, cv_ref, h * HD, 2 * kw + h * HD, HD)

    def fill_z(hs):
        for h in hs:
            s_hi, s_lo = split(state[h])
            kq = cat([k2[h // 2], q2[h // 2]], 0)
            zs[h] = mxu(cat([kq, kq[:, :HD]], 1), cat([s_hi, s_hi, s_lo], 0))

    half = vh // 2
    fills = [lambda: fill_q(pairs[: kh // 2]), lambda: fill_q(pairs[kh // 2 :]), lambda: fill_mix(pairs),
             lambda: fill_v(each[:half]), lambda: fill_v(each[half:]), lambda: fill_z(each)]
    invs = pair_inverses(lows, eye, left, fills)
    ts = []
    for inv in invs:
        ih, il = split(inv)
        rh, rl = split(pltpu.roll(inv, BLOCK, 1))
        for t in (jnp.where(left, ih, rl), jnp.where(left, rh, il)):
            ts.append(cat([t, t], 1))
    us = []
    for h in each:
        z = zs[h]
        right = cat([vs[h] - bs[h] * z[:BLOCK, :HD], -bs[h] * z[:BLOCK, HD:]], 1)
        r_hi, r_lo = split(right)
        us.append(mxu(ts[h], cat([r_hi, r_hi, r_lo, r_lo], 0)))
    for h in each:
        u_hi, u_lo = split(us[h])
        ds = mxu(km4[h // 2], cat([u_hi, u_hi, u_lo, u_lo], 0))
        o = gamma[:, h : h + 1] * (zs[h][BLOCK:] + ds[HD:])
        state[h] = last[:, h : h + 1] * (state[h] + ds[:HD])
        base_ref[here, h * HD : (h + 1) * HD] = o[:, :HD]
        o_hi, o_lo = split(o[:, HD:])
        map_ref[here, 2 * h * HD : (2 * h + 1) * HD] = o_hi
        map_ref[here, (2 * h + 1) * HD : (2 * h + 2) * HD] = o_lo

    @pl.when(n == pl.num_programs(0) - 1)
    def _():
        per = vh // 2
        for i in range(per):
            kept_ref[i] = state[pos[2] * per + i]
            away_ref[i] = state[(1 - pos[2]) * per + i]


def run_scan(pos, q, k, v, gc, bc, halo, cq, ck, cv):
    rows = q.shape[0]
    kw, vw = q.shape[1], v.shape[1]
    vh = vw // HD
    row_spec = lambda w: pl.BlockSpec((BLOCK, w), lambda n: (n, 0))
    full = lambda shape: pl.BlockSpec(shape, lambda n: (0,) * len(shape))
    half = (vh // 2, HD, 2 * HD)
    return pl.pallas_call(
        scan_kernel,
        grid=(rows // BLOCK,),
        in_specs=[pl.BlockSpec(memory_space=pltpu.SMEM), row_spec(kw), row_spec(kw), row_spec(vw),
                  full(gc.shape), full(bc.shape), full(halo.shape), full(cq.shape), full(ck.shape), full(cv.shape)],
        out_specs=[pl.BlockSpec(memory_space=pltpu.VMEM)] * 4,
        out_shape=[jax.ShapeDtypeStruct((rows, vw), F32), jax.ShapeDtypeStruct((rows, 2 * vw), BF16)]
        + [jax.ShapeDtypeStruct(half, F32)] * 2,
        scratch_shapes=[pltpu.VMEM((vh, HD, 2 * HD), F32), pltpu.VMEM((8, 2 * kw + vw), F32),
                        pltpu.VMEM((2, rows, vh), F32)],
        compiler_params=pltpu.CompilerParams(dimension_semantics=("arbitrary",), vmem_limit_bytes=10 << 20),
        name="scan",
    )(pos, q, k, v, gc, bc, halo, cq, ck, cv)


def dot3(a, b):
    a_hi, a_lo = split(a)
    b_hi, b_lo = split(b)
    return mxu(cat([a_hi, a_lo, a_hi], 1), cat([b_hi, b_hi, b_lo], 0))


def then(later, earlier):
    out = dot3(later[:, HD:], earlier)
    return cat([later[:, :HD] + out[:, :HD], out[:, HD:]], 1)


def vmem_call(body, outs, scratch, scalars, *arrays):
    return pl.pallas_call(
        body,
        in_specs=[pl.BlockSpec(memory_space=pltpu.SMEM)] + [pl.BlockSpec(memory_space=pltpu.VMEM)] * len(arrays),
        out_specs=[pl.BlockSpec(memory_space=pltpu.VMEM)] * len(outs),
        out_shape=[jax.ShapeDtypeStruct(s, F32) for s in outs],
        scratch_shapes=[pltpu.VMEM(s, F32) for s in scratch],
        compiler_params=pltpu.CompilerParams(vmem_limit_bytes=LIMIT),
    )(scalars, *arrays)


def pair_kernel(pos, kept, got, early_ref, o0, o1, o2, o3, both):
    first = pos[2] == 0
    for h in range(Z_CHIPS):
        mine, other = kept[h], got[h]
        early = jnp.where(first, mine, other)
        late = jnp.where(first, other, mine)
        early_ref[h] = early
        both[h] = then(late, early)
    for d, o in enumerate((o0, o1, o2, o3)):
        o[...] = both[(pos[1] + d) % Z_CHIPS]


def prefix_kernel(pos, a0, a1, a2, a3, pre_ref, tot_ref, line):
    z = pos[1]
    for d, a in enumerate((a0, a1, a2, a3)):
        line[(z - d + Z_CHIPS) % Z_CHIPS] = a[...]
    r = lax.broadcasted_iota(jnp.int32, (HD, 2 * HD), 0)
    c = lax.broadcasted_iota(jnp.int32, (HD, 2 * HD), 1)
    pre_ref[0] = jnp.where(r + HD == c, 1.0, 0.0).astype(F32)
    lower = line[0]
    middle = then(line[1], lower)
    pre_ref[1] = lower
    pre_ref[2] = middle
    pre_ref[3] = then(line[2], middle)
    tot_ref[...] = then(then(line[3], line[2]), middle)


def entry_kernel(pos, a0, a1, a2, a3, pre, o0, o1, o2, o3, line, states):
    x, z = pos[0], pos[1]
    for d, a in enumerate((a0, a1, a2, a3)):
        line[(x - d + X_CHIPS) % X_CHIPS] = a[...]
    run = jnp.zeros((HD, HD), F32)
    states[0] = run
    run = line[0, :, :HD]
    states[1] = run
    for i in range(2, X_CHIPS):
        run = line[i - 1, :, :HD] + dot3(line[i - 1, :, HD:], run)
        states[i] = run
    mine = states[x]
    for i in range(Z_CHIPS):
        states[i] = mine if i == 0 else pre[i, :, :HD] + dot3(pre[i, :, HD:], mine)
    for d, o in enumerate((o0, o1, o2, o3)):
        o[...] = states[(z + d) % Z_CHIPS]


def cores_kernel(pos, a0, a1, a2, a3, early, keep_ref, send_ref, line):
    z, first = pos[1], pos[2] == 0
    for d, a in enumerate((a0, a1, a2, a3)):
        line[(z - d + Z_CHIPS) % Z_CHIPS] = a[...]
    for h in range(Z_CHIPS):
        s = line[h]
        t = early[h, :, :HD] + dot3(early[h, :, HD:], s)
        keep_ref[h] = jnp.where(first, s, t)
        send_ref[h] = jnp.where(first, t, s)


def out_kernel(pos, base_ref, map_ref, s_ref, t_ref, gate_ref, gain_ref, o0, o1, o2, o3, rights, *, part):
    per = s_ref.shape[0]
    own = pos[2] == part
    for h in range(per):
        row = wide(jnp.where(own, s_ref[h], t_ref[h]))
        rights[h] = cat([row, row], 0)
    size = o0.shape[0]
    gain = gain_ref[...]
    for d, ref in enumerate((o0, o1, o2, o3)):
        rows = pl.ds(pl.multiple_of((pos[3] + d) % 4 * size, size), size)

        def step(h, _):
            at = (part * per + h) * HD
            cols = pl.ds(pl.multiple_of(at, HD), HD)
            o = base_ref[rows, cols] + fold(mxu(map_ref[rows, pl.ds(pl.multiple_of(2 * at, HD), 2 * HD)], rights[h]))
            g = gate_ref[rows, cols].astype(F32)
            y = o * lax.rsqrt(jnp.mean(o * o, -1, keepdims=True) + 1e-06) * gain * silu(g)
            ref[:, pl.ds(pl.multiple_of(h * HD, HD), HD)] = y.astype(BF16)
            return 0

        lax.fori_loop(0, per, step, 0)


def run_out(pos, base, maps, kept, got, gate, gain, part):
    rows = base.shape[0]
    per = kept.shape[0]
    vmem = pl.BlockSpec(memory_space=pltpu.VMEM)
    return pl.pallas_call(
        functools.partial(out_kernel, part=part),
        in_specs=[pl.BlockSpec(memory_space=pltpu.SMEM)] + [vmem] * 6,
        out_specs=[vmem] * 4,
        out_shape=[jax.ShapeDtypeStruct((rows // 4, per * HD), BF16)] * 4,
        scratch_shapes=[pltpu.VMEM((per, 2 * HD, 2 * HD), BF16)],
        compiler_params=pltpu.CompilerParams(vmem_limit_bytes=LIMIT),
    )(pos, base, maps, kept, got, gate, gain)


def project_kernel(pos, *refs, starts, picks, held, count, extra, final):
    ys, ws = refs[:count], refs[count : count + held]
    here, there = [ws[i] for i in picks[0]], [ws[i] for i in picks[1]]
    acc_ref = refs[count + held] if extra else None
    out_ref, *more = refs[count + held + extra :]
    depth = ys[0].shape[1]
    tile = 512
    tiles = out_ref.shape[1] // tile

    def sweep(ws):
        for t in range(tiles):
            cols = slice(t * tile, (t + 1) * tile)
            total = acc_ref[:, cols] if extra else None
            for p in range(count):
                term = mxu(ys[p][...], ws[p][starts[p] : starts[p] + depth, cols])
                total = term if total is None else total + term
            if final:
                more[0][t] = total.astype(BF16)
                store(t).start()
            else:
                out_ref[:, cols] = total

    def store(t):
        return pltpu.make_async_copy(more[0].at[t], out_ref.at[:, pl.ds(t * tile, tile)], more[1].at[t])

    if picks[0] == picks[1]:
        sweep(here)
    else:
        pl.when(pos[2] == 0)(lambda: sweep(here))
        pl.when(pos[2] != 0)(lambda: sweep(there))
    if final:
        for t in range(tiles):
            store(t).wait()


def project(pos, starts, ys, weights, picks, acc, dtype):
    rows, _ = ys[0].shape
    width = weights[0].shape[1]
    count = len(ys)
    final = dtype == BF16
    vmem, hbm = pl.BlockSpec(memory_space=pltpu.VMEM), pl.BlockSpec(memory_space=pl.ANY)
    accs = [] if acc is None else [acc]
    return pl.pallas_call(
        functools.partial(project_kernel, starts=starts, picks=picks, held=len(weights), count=count, extra=len(accs), final=final),
        in_specs=[pl.BlockSpec(memory_space=pltpu.SMEM)] + [vmem] * (count + len(weights) + len(accs)),
        out_specs=hbm if final else vmem,
        out_shape=jax.ShapeDtypeStruct((rows, width), dtype),
        scratch_shapes=[pltpu.VMEM((width // 512, rows, 512), dtype), pltpu.SemaphoreType.DMA((width // 512,))] * final,
        compiler_params=pltpu.CompilerParams(vmem_limit_bytes=14 << 20),
    )(pos, *ys, *weights, *accs)


def fetch_kernel(*refs):
    sem = refs[-1]
    copies = []
    for i in range(2):
        rows = refs[i].shape[0] // 4
        for j in range(4):
            part = pl.ds(j * rows, rows)
            copies.append(pltpu.make_async_copy(refs[i].at[part], refs[2 + i].at[part], sem.at[i, j]))
    for c in copies:
        c.start()
    for c in copies:
        c.wait()


def run_fetch(*arrays):
    return pl.pallas_call(
        fetch_kernel,
        in_specs=[pl.BlockSpec(memory_space=pl.ANY)] * 2,
        out_specs=[pl.BlockSpec(memory_space=pltpu.VMEM)] * 2,
        out_shape=[jax.ShapeDtypeStruct(a.shape, a.dtype) for a in arrays],
        scratch_shapes=[pltpu.SemaphoreType.DMA((2, 4))],
        compiler_params=pltpu.CompilerParams(vmem_limit_bytes=LIMIT),
        name="fetch",
    )(*arrays)


def rim_kernel(q, k, v, out_ref, sem):
    copies, at = [], 0
    for i, ref in enumerate((q, k, v)):
        rows, width = ref.shape
        copies.append(pltpu.make_async_copy(ref.at[pl.ds(rows - 8, 8)], out_ref.at[:, pl.ds(at, width)], sem.at[i]))
        at += width
    for c in copies:
        c.start()
    for c in copies:
        c.wait()


def run_rim(q, k, v):
    hbm = pl.BlockSpec(memory_space=pl.ANY)
    return pl.pallas_call(
        rim_kernel,
        in_specs=[hbm] * 3,
        out_specs=pl.BlockSpec(memory_space=pltpu.VMEM),
        out_shape=jax.ShapeDtypeStruct((8, q.shape[1] + k.shape[1] + v.shape[1]), BF16),
        scratch_shapes=[pltpu.SemaphoreType.DMA((3,))],
        name="rim",
    )(q, k, v)


def ctx_route(dx, dz, dc):
    def dest(i):
        x, z, c = i // (Z_CHIPS * CORES), (i // CORES) % Z_CHIPS, i % CORES
        return ((x + dx) % X_CHIPS * Z_CHIPS + (z + dz) % Z_CHIPS) * CORES + (c + dc) % CORES

    return [(i, dest(i)) for i in range(X_CHIPS * Z_CHIPS * CORES)]


def mesh_route(n_ctx, heads, moves):
    row = Z_CHIPS * CORES
    pairs = [(c, h) for c in range(n_ctx) for h in range(heads)]
    dest = lambda c, h, dx, dy: (c + dx * row) % n_ctx * heads + (h + dy) % heads
    return [(c * heads + h, dest(c, h, *moves[c % CORES])) for c, h in pairs]


def shards(query_raw, key_raw, value_raw, gate_branch, gate_code, beta_code,
           conv_query, conv_key, conv_value, norm_gain, out_weight):
    ctx = lax.axis_index("ctx")
    head = lax.axis_index("head")
    heads = lax.axis_size("head")
    x, z, core = ctx // (Z_CHIPS * CORES), (ctx // CORES) % Z_CHIPS, ctx % CORES
    pos = jnp.stack([x, z, core, head]).astype(jnp.int32)
    send = lambda a, dx, dz, dc: lax.ppermute(a, "ctx", ctx_route(dx, dz, dc))
    turn = lambda a, d: lax.ppermute(a, "head", [(i, (i + d) % heads) for i in range(heads)])
    hops = (1, 3, 2)
    barrier = lax.optimization_barrier

    n_ctx = lax.axis_size("ctx")
    raws = [pltpu.with_memory_space_constraint(a, pltpu.HBM) for a in (query_raw, key_raw, value_raw)]
    w_rows = out_weight.shape[0] // CORES
    halo = lax.ppermute(run_rim(*raws), "ctx", [(i, i + 1) for i in range(n_ctx - 1)])
    w_first = lax.ppermute(out_weight, ("ctx", "head"), mesh_route(n_ctx, heads, ((0, 2), (0, 1))))
    w_second = lax.ppermute(out_weight, ("ctx", "head"), mesh_route(n_ctx, heads, ((1, 0), (0, 3))))

    base, maps, kept, away = run_scan(pos, *raws, gate_code.T, beta_code.T, halo,
                                      conv_query, conv_key, conv_value)

    line, full = (HD, 2 * HD), (Z_CHIPS, HD, 2 * HD)
    early, *both = vmem_call(pair_kernel, [full] + [line] * 4, [full], pos, kept, send(away, 0, 0, 1))
    lines = [both[0]] + [send(both[d], 0, d, 0) for d in range(1, Z_CHIPS)]
    pre, tot = vmem_call(prefix_kernel, [full, line], [full], pos, *lines)
    tots = [tot] + [send(tot, d, 0, 0) for d in range(1, X_CHIPS)]
    entry = vmem_call(entry_kernel, [(HD, HD)] * 4, [full, (Z_CHIPS, HD, HD)], pos, *tots, pre)
    backs = [entry[0]] + [send(entry[d], 0, d, 0) for d in range(1, Z_CHIPS)]
    own, lent = vmem_call(cores_kernel, [(Z_CHIPS, HD, HD)] * 2, [(Z_CHIPS, HD, HD)], pos, *backs, early)
    got = send(lent, 0, 0, 1)

    gain = norm_gain.reshape(1, HD)
    y_a = run_out(pos, base, maps, own, got, gate_branch, gain, 0)
    a_got = [turn(y_a[d], d) for d in hops]
    y_b = run_out(pos, base, maps, own, got, gate_branch, gain, 1)
    b_got = [turn(y_b[d], d) for d in hops]
    _, w_first, w_second = barrier((y_b[0], w_first, w_second))
    swap_first, swap_second = send(w_first, 0, 0, 1), send(w_second, 0, 0, 1)
    acc = project(pos, (0, w_rows), [y_a[0], y_b[0]], [out_weight], ((0, 0),) * 2, None, F32)
    acc, w_first, w_second = barrier((acc, w_first, w_second))
    held = [*run_fetch(w_first, w_second), swap_first, swap_second]
    picks = ((2, 3, 0), (0, 1, 2))
    acc = project(pos, (0,) * 3, a_got, held, picks, acc, F32)
    return project(pos, (w_rows,) * 3, b_got, held, picks, acc, BF16)


def solution(mesh):
    return jax.shard_map(
        shards,
        mesh=mesh,
        in_specs=(P("ctx", "head"),) * 6 + (P(None, "head"),) * 3 + (P(), P("head", None)),
        out_specs=P(("ctx", "head"), None),
        check_vma=False,
    )
```

```python
import functools

import jax, jax.numpy as jnp
from jax import lax
from jax.experimental import pallas as pl
from jax.experimental.pallas import tpu as pltpu
from jax.sharding import PartitionSpec as P


Z_CHIPS, X_CHIPS, CORES = 4, 4, 2

F32, BF16 = jnp.float32, jnp.bfloat16
HD = 128
BLOCK = 64
KERNEL = 4
LIMIT = 6 << 20


def split(x):
    hi = x.astype(BF16)
    return hi, (x - hi.astype(F32)).astype(BF16)


def mxu(a, b):
    return jnp.dot(a, b, preferred_element_type=F32)


def cat(parts, axis):
    return jnp.concatenate(parts, axis)


def silu(x):
    return x / (1.0 + jnp.exp(-x))


def pair_rhs(y, left):
    hi, lo = split(y)
    zero = jnp.zeros_like(hi)
    hi = cat([jnp.where(left, hi, zero), jnp.where(left, zero, hi)], 0)
    lo = cat([jnp.where(left, lo, zero), jnp.where(left, zero, lo)], 0)
    row = cat([hi, lo], 1)
    return cat([row, row], 0)


def wide(x):
    return cat(split(x), 1)


def fold(out):
    return out[:, :HD] + out[:, HD:]


def pair_inverses(lows, eye, left, fills):
    raw = [mxu(wide(low), pair_rhs(low, left)) for low in lows]
    fills[0]()
    powers = [fold(r) for r in raw]
    invs = [eye - low for low in lows]
    for fill in fills[1:-1]:
        raw = [mxu(wide(cat([i, p], 0)), pair_rhs(p, left)) for i, p in zip(invs, powers)]
        fill()
        outs = [fold(r) for r in raw]
        invs = [i + o[:BLOCK] for i, o in zip(invs, outs)]
        powers = [o[BLOCK:] for o in outs]
    raw = [mxu(wide(i), pair_rhs(p, left)) for i, p in zip(invs, powers)]
    fills[-1]()
    return [i + fold(r) for i, r in zip(invs, raw)]


def conv(ext, taps):
    acc = None
    for j in range(KERNEL):
        s = KERNEL - 1 - j
        shifted = ext if s == 0 else pltpu.roll(ext, s, 0)
        term = taps[j : j + 1] * shifted[8:]
        acc = term if acc is None else acc + term
    return silu(acc)


def unit(x):
    return x * lax.rsqrt(jnp.sum(x * x, -1, keepdims=True) + 1e-06)


def scan_kernel(pos, q_ref, k_ref, v_ref, gc_ref, bc_ref, halo_ref, cq_ref, ck_ref, cv_ref,
                base_ref, map_ref, kept_ref, away_ref, state, carry, codes):
    n = pl.program_id(0)
    kh = q_ref.shape[1] // HD
    vh = v_ref.shape[1] // HD
    kw = kh * HD

    @pl.when(n == 0)
    def _():
        carry[...] = halo_ref[...].astype(F32)
        codes[0] = jnp.transpose(gc_ref[...].astype(F32))
        codes[1] = jnp.transpose(bc_ref[...].astype(F32))
        r = lax.broadcasted_iota(jnp.int32, (HD, 2 * HD), 0)
        c = lax.broadcasted_iota(jnp.int32, (HD, 2 * HD), 1)
        start = jnp.where(r + HD == c, 1.0, 0.0).astype(F32)
        for h in range(vh):
            state[h] = start

    rows = lax.broadcasted_iota(jnp.int32, (BLOCK, HD), 0)
    lanes = lax.broadcasted_iota(jnp.int32, (BLOCK, HD), 1)
    left = lanes < BLOCK
    cols = jnp.where(left, lanes, lanes - BLOCK)
    causal = rows >= cols
    strict = rows > cols
    eye = jnp.where(rows == cols, 1.0, 0.0).astype(F32)
    left_t = lax.broadcasted_iota(jnp.int32, (HD, HD), 1) < BLOCK

    here = pl.ds(pl.multiple_of(n * BLOCK, BLOCK), BLOCK)
    log_gate = jnp.log1p(-1e-06 * codes[0, here])
    tri = jnp.where(causal, 1.0, 0.0).astype(F32)[:, :BLOCK]
    cum = jnp.dot(tri, log_gate, precision=lax.Precision.HIGHEST, preferred_element_type=F32)
    gamma = jnp.exp(cum)
    beta = codes[1, here] / 1000.0
    beta_g = beta * jnp.exp(-cum)
    last = gamma[BLOCK - 1 :]

    def conved(ref, taps, src, dst, width):
        x = ref[:, src : src + width].astype(F32)
        ext = cat([carry[:, dst : dst + width], x], 0)
        carry[:, dst : dst + width] = x[BLOCK - 8 :]
        return conv(ext, taps[:, src : src + width].astype(F32))

    pairs = range(kh)
    each = range(vh)
    bs = [jnp.broadcast_to(beta[:, h : h + 1], (BLOCK, HD)) for h in each]
    kt2, k2, q2, lows = [], [], [None] * kh, []
    for j in pairs:
        k = unit(conved(k_ref, ck_ref, j * HD, kw + j * HD, HD))
        kt_hi, kt_lo = split(jnp.transpose(cat([k, k], 0)))
        kt2.append((kt_hi, kt_lo))
        k2.append(wide(k))
    for j in pairs:
        row = cat(kt2[j], 1)
        dots = fold(mxu(k2[j], cat([row, row], 0)))
        lows.append(jnp.where(strict, jnp.where(left, bs[2 * j], bs[2 * j + 1]) * dots, 0.0))
    km4, zs, vs = [None] * kh, [None] * vh, [None] * vh

    def fill_q(js):
        for j in js:
            q2[j] = wide(unit(conved(q_ref, cq_ref, j * HD, j * HD, HD)) * HD ** (-0.5))

    def fill_mix(js):
        for j in js:
            row = cat(kt2[j], 1)
            dots = fold(mxu(q2[j], cat([row, row], 0)))
            mh, ml = split(jnp.where(causal, dots, 0.0))
            km = cat([jnp.where(left_t, *kt2[j]), jnp.where(left, mh, ml)], 0)
            km4[j] = cat([km, km], 1)

    def fill_v(hs):
        for h in hs:
            vs[h] = beta_g[:, h : h + 1] * conved(v_ref, cv_ref, h * HD, 2 * kw + h * HD, HD)

    def fill_z(hs):
        for h in hs:
            s_hi, s_lo = split(state[h])
            kq = cat([k2[h // 2], q2[h // 2]], 0)
            zs[h] = mxu(cat([kq, kq[:, :HD]], 1), cat([s_hi, s_hi, s_lo], 0))

    half = vh // 2
    fills = [lambda: fill_q(pairs[: kh // 2]), lambda: fill_q(pairs[kh // 2 :]), lambda: fill_mix(pairs),
             lambda: fill_v(each[:half]), lambda: fill_v(each[half:]), lambda: fill_z(each)]
    invs = pair_inverses(lows, eye, left, fills)
    ts = []
    for inv in invs:
        ih, il = split(inv)
        rh, rl = split(pltpu.roll(inv, BLOCK, 1))
        for t in (jnp.where(left, ih, rl), jnp.where(left, rh, il)):
            ts.append(cat([t, t], 1))
    us = []
    for h in each:
        z = zs[h]
        right = cat([vs[h] - bs[h] * z[:BLOCK, :HD], -bs[h] * z[:BLOCK, HD:]], 1)
        r_hi, r_lo = split(right)
        us.append(mxu(ts[h], cat([r_hi, r_hi, r_lo, r_lo], 0)))
    for h in each:
        u_hi, u_lo = split(us[h])
        ds = mxu(km4[h // 2], cat([u_hi, u_hi, u_lo, u_lo], 0))
        o = gamma[:, h : h + 1] * (zs[h][BLOCK:] + ds[HD:])
        state[h] = last[:, h : h + 1] * (state[h] + ds[:HD])
        base_ref[here, h * HD : (h + 1) * HD] = o[:, :HD]
        o_hi, o_lo = split(o[:, HD:])
        map_ref[here, 2 * h * HD : (2 * h + 1) * HD] = o_hi
        map_ref[here, (2 * h + 1) * HD : (2 * h + 2) * HD] = o_lo

    @pl.when(n == pl.num_programs(0) - 1)
    def _():
        per = vh // 2
        for i in range(per):
            kept_ref[i] = state[pos[2] * per + i]
            away_ref[i] = state[(1 - pos[2]) * per + i]


def run_scan(pos, q, k, v, gc, bc, halo, cq, ck, cv):
    rows = q.shape[0]
    kw, vw = q.shape[1], v.shape[1]
    vh = vw // HD
    row_spec = lambda w: pl.BlockSpec((BLOCK, w), lambda n: (n, 0))
    full = lambda shape: pl.BlockSpec(shape, lambda n: (0,) * len(shape))
    half = (vh // 2, HD, 2 * HD)
    return pl.pallas_call(
        scan_kernel,
        grid=(rows // BLOCK,),
        in_specs=[pl.BlockSpec(memory_space=pltpu.SMEM), row_spec(kw), row_spec(kw), row_spec(vw),
                  full(gc.shape), full(bc.shape), full(halo.shape), full(cq.shape), full(ck.shape), full(cv.shape)],
        out_specs=[pl.BlockSpec(memory_space=pltpu.VMEM)] * 4,
        out_shape=[jax.ShapeDtypeStruct((rows, vw), F32), jax.ShapeDtypeStruct((rows, 2 * vw), BF16)]
        + [jax.ShapeDtypeStruct(half, F32)] * 2,
        scratch_shapes=[pltpu.VMEM((vh, HD, 2 * HD), F32), pltpu.VMEM((8, 2 * kw + vw), F32),
                        pltpu.VMEM((2, rows, vh), F32)],
        compiler_params=pltpu.CompilerParams(dimension_semantics=("arbitrary",), vmem_limit_bytes=10 << 20),
        name="scan",
    )(pos, q, k, v, gc, bc, halo, cq, ck, cv)


def dot3(a, b):
    a_hi, a_lo = split(a)
    b_hi, b_lo = split(b)
    return mxu(cat([a_hi, a_lo, a_hi], 1), cat([b_hi, b_hi, b_lo], 0))


def then(later, earlier):
    out = dot3(later[:, HD:], earlier)
    return cat([later[:, :HD] + out[:, :HD], out[:, HD:]], 1)


def vmem_call(body, outs, scratch, scalars, *arrays):
    return pl.pallas_call(
        body,
        in_specs=[pl.BlockSpec(memory_space=pltpu.SMEM)] + [pl.BlockSpec(memory_space=pltpu.VMEM)] * len(arrays),
        out_specs=[pl.BlockSpec(memory_space=pltpu.VMEM)] * len(outs),
        out_shape=[jax.ShapeDtypeStruct(s, F32) for s in outs],
        scratch_shapes=[pltpu.VMEM(s, F32) for s in scratch],
        compiler_params=pltpu.CompilerParams(vmem_limit_bytes=LIMIT),
    )(scalars, *arrays)


def pair_kernel(pos, kept, got, early_ref, o0, o1, o2, o3, both):
    first = pos[2] == 0
    for h in range(Z_CHIPS):
        mine, other = kept[h], got[h]
        early = jnp.where(first, mine, other)
        late = jnp.where(first, other, mine)
        early_ref[h] = early
        both[h] = then(late, early)
    for d, o in enumerate((o0, o1, o2, o3)):
        o[...] = both[(pos[1] + d) % Z_CHIPS]


def prefix_kernel(pos, a0, a1, a2, a3, pre_ref, tot_ref, line):
    z = pos[1]
    for d, a in enumerate((a0, a1, a2, a3)):
        line[(z - d + Z_CHIPS) % Z_CHIPS] = a[...]
    r = lax.broadcasted_iota(jnp.int32, (HD, 2 * HD), 0)
    c = lax.broadcasted_iota(jnp.int32, (HD, 2 * HD), 1)
    pre_ref[0] = jnp.where(r + HD == c, 1.0, 0.0).astype(F32)
    lower = line[0]
    middle = then(line[1], lower)
    pre_ref[1] = lower
    pre_ref[2] = middle
    pre_ref[3] = then(line[2], middle)
    tot_ref[...] = then(then(line[3], line[2]), middle)


def entry_kernel(pos, a0, a1, a2, a3, pre, o0, o1, o2, o3, line, states):
    x, z = pos[0], pos[1]
    for d, a in enumerate((a0, a1, a2, a3)):
        line[(x - d + X_CHIPS) % X_CHIPS] = a[...]
    run = jnp.zeros((HD, HD), F32)
    states[0] = run
    run = line[0, :, :HD]
    states[1] = run
    for i in range(2, X_CHIPS):
        run = line[i - 1, :, :HD] + dot3(line[i - 1, :, HD:], run)
        states[i] = run
    mine = states[x]
    for i in range(Z_CHIPS):
        states[i] = mine if i == 0 else pre[i, :, :HD] + dot3(pre[i, :, HD:], mine)
    for d, o in enumerate((o0, o1, o2, o3)):
        o[...] = states[(z + d) % Z_CHIPS]


def cores_kernel(pos, a0, a1, a2, a3, early, keep_ref, send_ref, line):
    z, first = pos[1], pos[2] == 0
    for d, a in enumerate((a0, a1, a2, a3)):
        line[(z - d + Z_CHIPS) % Z_CHIPS] = a[...]
    for h in range(Z_CHIPS):
        s = line[h]
        t = early[h, :, :HD] + dot3(early[h, :, HD:], s)
        keep_ref[h] = jnp.where(first, s, t)
        send_ref[h] = jnp.where(first, t, s)


def out_kernel(pos, base_ref, map_ref, s_ref, t_ref, gate_ref, gain_ref, o0, o1, o2, o3, rights, *, part):
    per = s_ref.shape[0]
    own = pos[2] == part
    for h in range(per):
        row = wide(jnp.where(own, s_ref[h], t_ref[h]))
        rights[h] = cat([row, row], 0)
    size = o0.shape[0]
    gain = gain_ref[...]
    for d, ref in enumerate((o0, o1, o2, o3)):
        rows = pl.ds(pl.multiple_of((pos[3] + d) % 4 * size, size), size)

        def step(h, _):
            at = (part * per + h) * HD
            cols = pl.ds(pl.multiple_of(at, HD), HD)
            o = base_ref[rows, cols] + fold(mxu(map_ref[rows, pl.ds(pl.multiple_of(2 * at, HD), 2 * HD)], rights[h]))
            g = gate_ref[rows, cols].astype(F32)
            y = o * lax.rsqrt(jnp.mean(o * o, -1, keepdims=True) + 1e-06) * gain * silu(g)
            ref[:, pl.ds(pl.multiple_of(h * HD, HD), HD)] = y.astype(BF16)
            return 0

        lax.fori_loop(0, per, step, 0)


def run_out(pos, base, maps, kept, got, gate, gain, part):
    rows = base.shape[0]
    per = kept.shape[0]
    vmem = pl.BlockSpec(memory_space=pltpu.VMEM)
    return pl.pallas_call(
        functools.partial(out_kernel, part=part),
        in_specs=[pl.BlockSpec(memory_space=pltpu.SMEM)] + [vmem] * 6,
        out_specs=[vmem] * 4,
        out_shape=[jax.ShapeDtypeStruct((rows // 4, per * HD), BF16)] * 4,
        scratch_shapes=[pltpu.VMEM((per, 2 * HD, 2 * HD), BF16)],
        compiler_params=pltpu.CompilerParams(vmem_limit_bytes=LIMIT),
    )(pos, base, maps, kept, got, gate, gain)


def own_kernel(ya, yb, w, out_ref):
    depth = ya.shape[1]
    for c in range(0, out_ref.shape[1], 512):
        cols = slice(c, c + 512)
        out_ref[:, cols] = mxu(ya[...], w[:depth, cols]) + mxu(yb[...], w[depth:, cols])


def run_own(ya, yb, weight):
    vmem = pl.BlockSpec(memory_space=pltpu.VMEM)
    return pl.pallas_call(
        own_kernel,
        in_specs=[vmem] * 3,
        out_specs=vmem,
        out_shape=jax.ShapeDtypeStruct((ya.shape[0], weight.shape[1]), F32),
        compiler_params=pltpu.CompilerParams(vmem_limit_bytes=LIMIT),
        name="own",
    )(ya, yb, weight)


def project_kernel(pos, y1, y3, y2, mine, theirs, q_mine, n_mine, q_theirs, n_theirs, acc_ref, out_ref, *more,
                   part, final):
    depth, tile = y1.shape[1], 512
    tiles = out_ref.shape[1] // tile
    rows = slice(part * depth, (part + 1) * depth)
    size = q_mine.shape[0]
    parity = pos[part] % 2
    first = pl.ds(pl.multiple_of(parity * size, size), size)
    second = pl.ds(pl.multiple_of((1 - parity) * size, size), size)

    def store(t):
        return pltpu.make_async_copy(more[0].at[t], out_ref.at[:, pl.ds(t * tile, tile)], more[1].at[t])

    def sweep(w1, w3, near, far):
        for t in range(tiles):
            cols = slice(t * tile, (t + 1) * tile)
            total = acc_ref[:, cols] + mxu(y1[...], w1[rows, cols]) + mxu(y3[...], w3[rows, cols])
            total = total + mxu(y2[:, first], near[:, cols]) + mxu(y2[:, second], far[:, cols])
            if final:
                more[0][t] = total.astype(BF16)
                store(t).start()
            else:
                out_ref[:, cols] = total

    for core, (w1, w3) in enumerate(((mine, theirs), (theirs, mine))):
        near, far = (q_mine, n_mine) if core == part else (q_theirs, n_theirs)
        pl.when(pos[2] == core)(functools.partial(sweep, w1, w3, near, far))
    if final:
        for t in range(tiles):
            store(t).wait()


def project(pos, part, ys, weights, acc, final):
    rows, width = acc.shape
    vmem, hbm = pl.BlockSpec(memory_space=pltpu.VMEM), pl.BlockSpec(memory_space=pl.ANY)
    dtype = BF16 if final else F32
    return pl.pallas_call(
        functools.partial(project_kernel, part=part, final=final),
        in_specs=[pl.BlockSpec(memory_space=pltpu.SMEM)] + [vmem] * 10,
        out_specs=hbm if final else vmem,
        out_shape=jax.ShapeDtypeStruct((rows, width), dtype),
        scratch_shapes=[pltpu.VMEM((width // 512, rows, 512), dtype), pltpu.SemaphoreType.DMA((width // 512,))] * final,
        compiler_params=pltpu.CompilerParams(vmem_limit_bytes=14 << 20),
    )(pos, *ys, *weights, acc)


def quarter_kernel(pos, w, out_ref, sem):
    rows = out_ref.shape[0]
    side = jnp.where(pos[2] == 0, pos[0], pos[1]) % 2
    top = pl.multiple_of((pos[2] * 2 + side) * rows, rows)
    piece = rows // 4
    copies = [pltpu.make_async_copy(w.at[pl.ds(top + i * piece, piece)], out_ref.at[pl.ds(i * piece, piece)], sem.at[i])
              for i in range(4)]
    for c in copies:
        c.start()
    for c in copies:
        c.wait()


def run_quarter(pos, weight):
    return pl.pallas_call(
        quarter_kernel,
        in_specs=[pl.BlockSpec(memory_space=pltpu.SMEM), pl.BlockSpec(memory_space=pl.ANY)],
        out_specs=pl.BlockSpec(memory_space=pltpu.VMEM),
        out_shape=jax.ShapeDtypeStruct((weight.shape[0] // 4, weight.shape[1]), BF16),
        scratch_shapes=[pltpu.SemaphoreType.DMA((4,))],
        compiler_params=pltpu.CompilerParams(vmem_limit_bytes=LIMIT),
        name="quarter",
    )(pos, weight)


def fetch_kernel(w, out_ref, sem):
    rows = w.shape[0] // 8
    parts = [pl.ds(i * rows, rows) for i in range(8)]
    copies = [pltpu.make_async_copy(w.at[p], out_ref.at[p], sem.at[i]) for i, p in enumerate(parts)]
    for c in copies:
        c.start()
    for c in copies:
        c.wait()


def run_fetch(w):
    return pl.pallas_call(
        fetch_kernel,
        in_specs=[pl.BlockSpec(memory_space=pl.ANY)],
        out_specs=pl.BlockSpec(memory_space=pltpu.VMEM),
        out_shape=jax.ShapeDtypeStruct(w.shape, w.dtype),
        scratch_shapes=[pltpu.SemaphoreType.DMA((8,))],
        compiler_params=pltpu.CompilerParams(vmem_limit_bytes=LIMIT),
        name="fetch",
    )(w)


def rim_kernel(q, k, v, out_ref, sem):
    copies, at = [], 0
    for i, ref in enumerate((q, k, v)):
        rows, width = ref.shape
        copies.append(pltpu.make_async_copy(ref.at[pl.ds(rows - 8, 8)], out_ref.at[:, pl.ds(at, width)], sem.at[i]))
        at += width
    for c in copies:
        c.start()
    for c in copies:
        c.wait()


def run_rim(q, k, v):
    hbm = pl.BlockSpec(memory_space=pl.ANY)
    return pl.pallas_call(
        rim_kernel,
        in_specs=[hbm] * 3,
        out_specs=pl.BlockSpec(memory_space=pltpu.VMEM),
        out_shape=jax.ShapeDtypeStruct((8, q.shape[1] + k.shape[1] + v.shape[1]), BF16),
        scratch_shapes=[pltpu.SemaphoreType.DMA((3,))],
        compiler_params=pltpu.CompilerParams(vmem_limit_bytes=LIMIT),
        name="rim",
    )(q, k, v)


def ctx_route(dx, dz, dc):
    def dest(i):
        x, z, c = i // (Z_CHIPS * CORES), (i // CORES) % Z_CHIPS, i % CORES
        return ((x + dx) % X_CHIPS * Z_CHIPS + (z + dz) % Z_CHIPS) * CORES + (c + dc) % CORES

    return [(i, dest(i)) for i in range(X_CHIPS * Z_CHIPS * CORES)]


def mesh_route(n_ctx, heads, turns):
    pairs = [(c, h) for c in range(n_ctx) for h in range(heads)]
    return [(c * heads + h, c * heads + (h + turns[c % CORES]) % heads) for c, h in pairs]


def beside_route(n_ctx):
    flip = (Z_CHIPS * CORES, CORES)
    return [(c, c ^ flip[c % CORES]) for c in range(n_ctx)]


def shards(query_raw, key_raw, value_raw, gate_branch, gate_code, beta_code,
           conv_query, conv_key, conv_value, norm_gain, out_weight):
    ctx = lax.axis_index("ctx")
    head = lax.axis_index("head")
    heads = lax.axis_size("head")
    x, z, core = ctx // (Z_CHIPS * CORES), (ctx // CORES) % Z_CHIPS, ctx % CORES
    pos = jnp.stack([x, z, core, head]).astype(jnp.int32)
    send = lambda a, dx, dz, dc: lax.ppermute(a, "ctx", ctx_route(dx, dz, dc))
    turn = lambda a, d: lax.ppermute(a, "head", [(i, (i + d) % heads) for i in range(heads)])
    hops = (1, 3, 2)
    barrier = lax.optimization_barrier

    n_ctx = lax.axis_size("ctx")
    raws = [pltpu.with_memory_space_constraint(a, pltpu.HBM) for a in (query_raw, key_raw, value_raw)]
    halo = lax.ppermute(run_rim(*raws), "ctx", [(i, i + 1) for i in range(n_ctx - 1)])
    w_full = lax.ppermute(out_weight, ("ctx", "head"), mesh_route(n_ctx, heads, (1, 3)))
    w_near = turn(run_quarter(pos, out_weight), 2)

    base, maps, kept, away = run_scan(pos, *raws, gate_code.T, beta_code.T, halo,
                                      conv_query, conv_key, conv_value)

    line, full = (HD, 2 * HD), (Z_CHIPS, HD, 2 * HD)
    early, *both = vmem_call(pair_kernel, [full] + [line] * 4, [full], pos, kept, send(away, 0, 0, 1))
    *both, w_local = barrier((*both, out_weight))
    lines = [both[0]] + [send(both[d], 0, d, 0) for d in range(1, Z_CHIPS)]
    *lines, w_local = barrier((*lines, run_fetch(w_local)))
    pre, tot = vmem_call(prefix_kernel, [full, line], [full], pos, *lines)
    tots = [tot] + [send(tot, d, 0, 0) for d in range(1, X_CHIPS)]
    entry = vmem_call(entry_kernel, [(HD, HD)] * 4, [full, (Z_CHIPS, HD, HD)], pos, *tots, pre)
    backs = [entry[0]] + [send(entry[d], 0, d, 0) for d in range(1, Z_CHIPS)]
    own, lent = vmem_call(cores_kernel, [(Z_CHIPS, HD, HD)] * 2, [(Z_CHIPS, HD, HD)], pos, *backs, early)
    got = send(lent, 0, 0, 1)

    gain = norm_gain.reshape(1, HD)
    y_a = run_out(pos, base, maps, own, got, gate_branch, gain, 0)
    a_got = [turn(y_a[d], d) for d in hops]
    _, w_full, w_near = barrier((y_a[0], w_full, w_near))
    w_far = lax.ppermute(w_near, "ctx", beside_route(n_ctx))
    near_there, full_there = send(w_near, 0, 0, 1), send(w_full, 0, 0, 1)
    y_b = run_out(pos, base, maps, own, got, gate_branch, gain, 1)
    b_got = [turn(y_b[d], d) for d in hops]
    acc = run_own(y_a[0], y_b[0], w_local)
    acc, w_far = barrier((acc, w_far))
    far_there = send(w_far, 0, 0, 1)
    acc, w_kept = barrier((acc, w_full))
    weights = [run_fetch(w_kept), full_there, w_near, w_far, near_there, far_there]
    acc = project(pos, 0, a_got, weights, acc, False)
    return project(pos, 1, b_got, weights, acc, True)


def solution(mesh):
    return jax.shard_map(
        shards,
        mesh=mesh,
        in_specs=(P("ctx", "head"),) * 6 + (P(None, "head"),) * 3 + (P(), P("head", None)),
        out_specs=P(("ctx", "head"), None),
        check_vma=False,
    )
```

```python
import functools

import jax, jax.numpy as jnp
from jax import lax
from jax.experimental import pallas as pl
from jax.experimental.pallas import tpu as pltpu
from jax.sharding import PartitionSpec as P


Z_CHIPS, X_CHIPS, CORES = 4, 4, 2

F32, BF16 = jnp.float32, jnp.bfloat16
HD = 128
BLOCK = 64
LIMIT = 6 << 20


def split(x):
    hi = x.astype(BF16)
    return hi, (x - hi.astype(F32)).astype(BF16)


def mxu(a, b):
    return jnp.dot(a, b, preferred_element_type=F32)


def cat(parts, axis):
    return jnp.concatenate(parts, axis)


def silu(x):
    return x / (1.0 + jnp.exp(-x))


def pair_rhs(y, left):
    hi, lo = split(y)
    zero = jnp.zeros_like(hi)
    hi = cat([jnp.where(left, hi, zero), jnp.where(left, zero, hi)], 0)
    lo = cat([jnp.where(left, lo, zero), jnp.where(left, zero, lo)], 0)
    row = cat([hi, lo], 1)
    return cat([row, row], 0)


def wide(x):
    return cat(split(x), 1)


def fold(out):
    return out[:, :HD] + out[:, HD:]


def pair_inverses(lows, eye, left, fills):
    raw = [mxu(wide(low), pair_rhs(low, left)) for low in lows]
    fills[0]()
    powers = [fold(r) for r in raw]
    invs = [eye - low for low in lows]
    for fill in fills[1:-1]:
        raw = [mxu(wide(cat([i, p], 0)), pair_rhs(p, left)) for i, p in zip(invs, powers)]
        fill()
        outs = [fold(r) for r in raw]
        invs = [i + o[:BLOCK] for i, o in zip(invs, outs)]
        powers = [o[BLOCK:] for o in outs]
    raw = [mxu(wide(i), pair_rhs(p, left)) for i, p in zip(invs, powers)]
    fills[-1]()
    return [i + fold(r) for i, r in zip(invs, raw)]


def conv(ext, taps):
    older = taps[0:1] * pltpu.roll(ext, 1, 0) + taps[1:2] * ext
    newer = taps[2:3] * pltpu.roll(ext, 1, 0) + taps[3:4] * ext
    return silu((pltpu.roll(older, 2, 0) + newer)[8:])


def unit(x):
    return x * lax.rsqrt(jnp.sum(x * x, -1, keepdims=True) + 1e-06)


def scan_kernel(pos, q_ref, k_ref, v_ref, gc_ref, bc_ref, halo_ref, cq_ref, ck_ref, cv_ref,
                base_ref, map_ref, kept_ref, away_ref, state, carry, codes):
    n = pl.program_id(0)
    kh = q_ref.shape[1] // HD
    vh = v_ref.shape[1] // HD
    kw = kh * HD

    @pl.when(n == 0)
    def _():
        carry[...] = halo_ref[...].astype(F32)
        codes[0] = jnp.transpose(gc_ref[...].astype(F32))
        codes[1] = jnp.transpose(bc_ref[...].astype(F32))
        r = lax.broadcasted_iota(jnp.int32, (HD, 2 * HD), 0)
        c = lax.broadcasted_iota(jnp.int32, (HD, 2 * HD), 1)
        start = jnp.where(r + HD == c, 1.0, 0.0).astype(F32)
        for h in range(vh):
            state[h] = start

    rows = lax.broadcasted_iota(jnp.int32, (BLOCK, HD), 0)
    lanes = lax.broadcasted_iota(jnp.int32, (BLOCK, HD), 1)
    left = lanes < BLOCK
    cols = jnp.where(left, lanes, lanes - BLOCK)
    causal = rows >= cols
    strict = rows > cols
    eye = jnp.where(rows == cols, 1.0, 0.0).astype(F32)
    left_t = lax.broadcasted_iota(jnp.int32, (HD, HD), 1) < BLOCK

    here = pl.ds(pl.multiple_of(n * BLOCK, BLOCK), BLOCK)
    log_gate = jnp.log1p(-1e-06 * codes[0, here])
    tri = jnp.where(causal, 1.0, 0.0).astype(F32)[:, :BLOCK]
    cum = jnp.dot(tri, log_gate, precision=lax.Precision.HIGHEST, preferred_element_type=F32)
    gamma = jnp.exp(cum)
    beta = codes[1, here] / 1000.0
    beta_g = beta * jnp.exp(-cum)
    last = gamma[BLOCK - 1 :]

    def conved(ref, taps, src, dst, width):
        x = ref[:, src : src + width].astype(F32)
        ext = cat([carry[:, dst : dst + width], x], 0)
        carry[:, dst : dst + width] = x[BLOCK - 8 :]
        return conv(ext, taps[:, src : src + width].astype(F32))

    pairs = range(kh)
    each = range(vh)
    bs = [jnp.broadcast_to(beta[:, h : h + 1], (BLOCK, HD)) for h in each]
    kt2, k2, q2, lows = [], [], [None] * kh, []
    for j in pairs:
        k = unit(conved(k_ref, ck_ref, j * HD, kw + j * HD, HD))
        kt_hi, kt_lo = split(jnp.transpose(cat([k, k], 0)))
        kt2.append((kt_hi, kt_lo))
        k2.append(wide(k))
    for j in pairs:
        row = cat(kt2[j], 1)
        dots = fold(mxu(k2[j], cat([row, row], 0)))
        lows.append(jnp.where(strict, jnp.where(left, bs[2 * j], bs[2 * j + 1]) * dots, 0.0))
    km4, zs, vs = [None] * kh, [None] * vh, [None] * vh

    def fill_q(js):
        for j in js:
            q2[j] = wide(unit(conved(q_ref, cq_ref, j * HD, j * HD, HD)) * HD ** (-0.5))

    def fill_mix(js):
        for j in js:
            row = cat(kt2[j], 1)
            dots = fold(mxu(q2[j], cat([row, row], 0)))
            mh, ml = split(jnp.where(causal, dots, 0.0))
            km = cat([jnp.where(left_t, *kt2[j]), jnp.where(left, mh, ml)], 0)
            km4[j] = cat([km, km], 1)

    def fill_v(hs):
        for h in hs:
            vs[h] = beta_g[:, h : h + 1] * conved(v_ref, cv_ref, h * HD, 2 * kw + h * HD, HD)

    def fill_z(hs):
        for h in hs:
            s_hi, s_lo = split(state[h])
            kq = cat([k2[h // 2], q2[h // 2]], 0)
            zs[h] = mxu(cat([kq, kq[:, :HD]], 1), cat([s_hi, s_hi, s_lo], 0))

    half = vh // 2
    fills = [lambda: fill_q(pairs[: kh // 2]), lambda: fill_q(pairs[kh // 2 :]), lambda: fill_mix(pairs),
             lambda: fill_v(each[:half]), lambda: fill_v(each[half:]), lambda: fill_z(each)]
    invs = pair_inverses(lows, eye, left, fills)
    ts = []
    for inv in invs:
        ih, il = split(inv)
        rh, rl = split(pltpu.roll(inv, BLOCK, 1))
        for t in (jnp.where(left, ih, rl), jnp.where(left, rh, il)):
            ts.append(cat([t, t], 1))
    us = []
    for h in each:
        z = zs[h]
        right = cat([vs[h] - bs[h] * z[:BLOCK, :HD], -bs[h] * z[:BLOCK, HD:]], 1)
        r_hi, r_lo = split(right)
        us.append(mxu(ts[h], cat([r_hi, r_hi, r_lo, r_lo], 0)))
    for h in each:
        u_hi, u_lo = split(us[h])
        ds = mxu(km4[h // 2], cat([u_hi, u_hi, u_lo, u_lo], 0))
        o = gamma[:, h : h + 1] * (zs[h][BLOCK:] + ds[HD:])
        state[h] = last[:, h : h + 1] * (state[h] + ds[:HD])
        base_ref[here, h * HD : (h + 1) * HD] = o[:, :HD]
        o_hi, o_lo = split(o[:, HD:])
        map_ref[here, 2 * h * HD : (2 * h + 1) * HD] = o_hi
        map_ref[here, (2 * h + 1) * HD : (2 * h + 2) * HD] = o_lo

    @pl.when(n == pl.num_programs(0) - 1)
    def _():
        per = vh // 2
        for i in range(per):
            kept_ref[i] = state[pos[2] * per + i]
            away_ref[i] = state[(1 - pos[2]) * per + i]


def run_scan(pos, q, k, v, gc, bc, halo, cq, ck, cv):
    rows = q.shape[0]
    kw, vw = q.shape[1], v.shape[1]
    vh = vw // HD
    row_spec = lambda w: pl.BlockSpec((BLOCK, w), lambda n: (n, 0))
    full = lambda shape: pl.BlockSpec(shape, lambda n: (0,) * len(shape))
    half = (vh // 2, HD, 2 * HD)
    return pl.pallas_call(
        scan_kernel,
        grid=(rows // BLOCK,),
        in_specs=[pl.BlockSpec(memory_space=pltpu.SMEM), row_spec(kw), row_spec(kw), row_spec(vw),
                  full(gc.shape), full(bc.shape), full(halo.shape), full(cq.shape), full(ck.shape), full(cv.shape)],
        out_specs=[pl.BlockSpec(memory_space=pltpu.VMEM)] * 4,
        out_shape=[jax.ShapeDtypeStruct((rows, vw), F32), jax.ShapeDtypeStruct((rows, 2 * vw), BF16)]
        + [jax.ShapeDtypeStruct(half, F32)] * 2,
        scratch_shapes=[pltpu.VMEM((vh, HD, 2 * HD), F32), pltpu.VMEM((8, 2 * kw + vw), F32),
                        pltpu.VMEM((2, rows, vh), F32)],
        compiler_params=pltpu.CompilerParams(dimension_semantics=("arbitrary",), vmem_limit_bytes=10 << 20),
        name="scan",
    )(pos, q, k, v, gc, bc, halo, cq, ck, cv)


def dot3(a, b):
    a_hi, a_lo = split(a)
    b_hi, b_lo = split(b)
    return mxu(cat([a_hi, a_lo, a_hi], 1), cat([b_hi, b_hi, b_lo], 0))


def then(later, earlier):
    out = dot3(later[:, HD:], earlier)
    return cat([later[:, :HD] + out[:, :HD], out[:, HD:]], 1)


def vmem_call(body, outs, scratch, scalars, *arrays):
    return pl.pallas_call(
        body,
        in_specs=[pl.BlockSpec(memory_space=pltpu.SMEM)] + [pl.BlockSpec(memory_space=pltpu.VMEM)] * len(arrays),
        out_specs=[pl.BlockSpec(memory_space=pltpu.VMEM)] * len(outs),
        out_shape=[jax.ShapeDtypeStruct(s, F32) for s in outs],
        scratch_shapes=[pltpu.VMEM(s, F32) for s in scratch],
        compiler_params=pltpu.CompilerParams(vmem_limit_bytes=LIMIT),
    )(scalars, *arrays)


def pair_kernel(pos, kept, got, early_ref, o0, o1, o2, o3, both):
    first = pos[2] == 0
    for h in range(Z_CHIPS):
        mine, other = kept[h], got[h]
        early = jnp.where(first, mine, other)
        late = jnp.where(first, other, mine)
        early_ref[h] = early
        both[h] = then(late, early)
    for d, o in enumerate((o0, o1, o2, o3)):
        o[...] = both[(pos[1] + d) % Z_CHIPS]


def prefix_kernel(pos, a0, a1, a2, a3, pre_ref, tot_ref, line):
    z = pos[1]
    for d, a in enumerate((a0, a1, a2, a3)):
        line[(z - d + Z_CHIPS) % Z_CHIPS] = a[...]
    r = lax.broadcasted_iota(jnp.int32, (HD, 2 * HD), 0)
    c = lax.broadcasted_iota(jnp.int32, (HD, 2 * HD), 1)
    pre_ref[0] = jnp.where(r + HD == c, 1.0, 0.0).astype(F32)
    lower = line[0]
    middle = then(line[1], lower)
    pre_ref[1] = lower
    pre_ref[2] = middle
    pre_ref[3] = then(line[2], middle)
    tot_ref[...] = then(then(line[3], line[2]), middle)


def entry_kernel(pos, a0, a1, a2, a3, pre, o0, o1, o2, o3, line, states):
    x, z = pos[0], pos[1]
    for d, a in enumerate((a0, a1, a2, a3)):
        line[(x - d + X_CHIPS) % X_CHIPS] = a[...]
    run = jnp.zeros((HD, HD), F32)
    states[0] = run
    run = line[0, :, :HD]
    states[1] = run
    for i in range(2, X_CHIPS):
        run = line[i - 1, :, :HD] + dot3(line[i - 1, :, HD:], run)
        states[i] = run
    mine = states[x]
    for i in range(Z_CHIPS):
        states[i] = mine if i == 0 else pre[i, :, :HD] + dot3(pre[i, :, HD:], mine)
    for d, o in enumerate((o0, o1, o2, o3)):
        o[...] = states[(z + d) % Z_CHIPS]


def cores_kernel(pos, a0, a1, a2, a3, early, keep_ref, send_ref, line):
    z, first = pos[1], pos[2] == 0
    for d, a in enumerate((a0, a1, a2, a3)):
        line[(z - d + Z_CHIPS) % Z_CHIPS] = a[...]
    for h in range(Z_CHIPS):
        s = line[h]
        t = early[h, :, :HD] + dot3(early[h, :, HD:], s)
        keep_ref[h] = jnp.where(first, s, t)
        send_ref[h] = jnp.where(first, t, s)


def out_kernel(pos, base_ref, map_ref, s_ref, t_ref, gate_ref, gain_ref, o0, o1, o2, o3, rights, *, part):
    per = s_ref.shape[0]
    own = pos[2] == part
    for h in range(per):
        row = wide(jnp.where(own, s_ref[h], t_ref[h]))
        rights[h] = cat([row, row], 0)
    size = o0.shape[0]
    gain = gain_ref[...]
    for d, ref in enumerate((o0, o1, o2, o3)):
        rows = pl.ds(pl.multiple_of((pos[3] + d) % 4 * size, size), size)

        def step(h, _):
            at = (part * per + h) * HD
            cols = pl.ds(pl.multiple_of(at, HD), HD)
            o = base_ref[rows, cols] + fold(mxu(map_ref[rows, pl.ds(pl.multiple_of(2 * at, HD), 2 * HD)], rights[h]))
            g = gate_ref[rows, cols].astype(F32)
            y = o * lax.rsqrt(jnp.mean(o * o, -1, keepdims=True) + 1e-06) * gain * silu(g)
            ref[:, pl.ds(pl.multiple_of(h * HD, HD), HD)] = y.astype(BF16)
            return 0

        lax.fori_loop(0, per, step, 0, unroll=2)


def run_out(pos, base, maps, kept, got, gate, gain, part):
    rows = base.shape[0]
    per = kept.shape[0]
    vmem = pl.BlockSpec(memory_space=pltpu.VMEM)
    return pl.pallas_call(
        functools.partial(out_kernel, part=part),
        in_specs=[pl.BlockSpec(memory_space=pltpu.SMEM)] + [vmem] * 6,
        out_specs=[vmem] * 4,
        out_shape=[jax.ShapeDtypeStruct((rows // 4, per * HD), BF16)] * 4,
        scratch_shapes=[pltpu.VMEM((per, 2 * HD, 2 * HD), BF16)],
        compiler_params=pltpu.CompilerParams(vmem_limit_bytes=LIMIT),
    )(pos, base, maps, kept, got, gate, gain)


def own_kernel(ya, yb, w, out_ref):
    depth = ya.shape[1]
    for c in range(0, out_ref.shape[1], 512):
        cols = slice(c, c + 512)
        out_ref[:, cols] = mxu(ya[...], w[:depth, cols]) + mxu(yb[...], w[depth:, cols])


def run_own(ya, yb, weight):
    vmem = pl.BlockSpec(memory_space=pltpu.VMEM)
    return pl.pallas_call(
        own_kernel,
        in_specs=[vmem] * 3,
        out_specs=vmem,
        out_shape=jax.ShapeDtypeStruct((ya.shape[0], weight.shape[1]), F32),
        compiler_params=pltpu.CompilerParams(vmem_limit_bytes=LIMIT),
        name="own",
    )(ya, yb, weight)


def project_kernel(pos, y1, y3, y2, mine, theirs, q_mine, n_mine, q_theirs, n_theirs, acc_ref, out_ref, *more,
                   part, final):
    depth, tile = y1.shape[1], 512
    tiles = out_ref.shape[1] // tile
    rows = slice(part * depth, (part + 1) * depth)
    size = q_mine.shape[0]
    parity = pos[part] % 2
    first = pl.ds(pl.multiple_of(parity * size, size), size)
    second = pl.ds(pl.multiple_of((1 - parity) * size, size), size)

    def store(t):
        return pltpu.make_async_copy(more[0].at[t], out_ref.at[:, pl.ds(t * tile, tile)], more[1].at[t])

    def sweep(w1, w3, near, far):
        for t in range(tiles):
            cols = slice(t * tile, (t + 1) * tile)
            total = acc_ref[:, cols] + mxu(y1[...], w1[rows, cols]) + mxu(y3[...], w3[rows, cols])
            total = total + mxu(y2[:, first], near[:, cols]) + mxu(y2[:, second], far[:, cols])
            if final:
                more[0][t] = total.astype(BF16)
                store(t).start()
            else:
                out_ref[:, cols] = total

    for core, (w1, w3) in enumerate(((mine, theirs), (theirs, mine))):
        near, far = (q_mine, n_mine) if core == part else (q_theirs, n_theirs)
        pl.when(pos[2] == core)(functools.partial(sweep, w1, w3, near, far))
    if final:
        for t in range(tiles):
            store(t).wait()


def project(pos, part, ys, weights, acc, final):
    rows, width = acc.shape
    vmem, hbm = pl.BlockSpec(memory_space=pltpu.VMEM), pl.BlockSpec(memory_space=pl.ANY)
    dtype = BF16 if final else F32
    return pl.pallas_call(
        functools.partial(project_kernel, part=part, final=final),
        in_specs=[pl.BlockSpec(memory_space=pltpu.SMEM)] + [vmem] * 10,
        out_specs=hbm if final else vmem,
        out_shape=jax.ShapeDtypeStruct((rows, width), dtype),
        scratch_shapes=[pltpu.VMEM((width // 512, rows, 512), dtype), pltpu.SemaphoreType.DMA((width // 512,))] * final,
        compiler_params=pltpu.CompilerParams(vmem_limit_bytes=14 << 20),
    )(pos, *ys, *weights, acc)


def quarter_kernel(pos, w, out_ref, sem):
    rows = out_ref.shape[0]
    side = jnp.where(pos[2] == 0, pos[0], pos[1]) % 2
    top = pl.multiple_of((pos[2] * 2 + side) * rows, rows)
    piece = rows // 4
    copies = [pltpu.make_async_copy(w.at[pl.ds(top + i * piece, piece)], out_ref.at[pl.ds(i * piece, piece)], sem.at[i])
              for i in range(4)]
    for c in copies:
        c.start()
    for c in copies:
        c.wait()


def run_quarter(pos, weight):
    return pl.pallas_call(
        quarter_kernel,
        in_specs=[pl.BlockSpec(memory_space=pltpu.SMEM), pl.BlockSpec(memory_space=pl.ANY)],
        out_specs=pl.BlockSpec(memory_space=pltpu.VMEM),
        out_shape=jax.ShapeDtypeStruct((weight.shape[0] // 4, weight.shape[1]), BF16),
        scratch_shapes=[pltpu.SemaphoreType.DMA((4,))],
        compiler_params=pltpu.CompilerParams(vmem_limit_bytes=LIMIT),
        name="quarter",
    )(pos, weight)


def fetch_kernel(w, out_ref, sem):
    rows = w.shape[0] // 8
    parts = [pl.ds(i * rows, rows) for i in range(8)]
    copies = [pltpu.make_async_copy(w.at[p], out_ref.at[p], sem.at[i]) for i, p in enumerate(parts)]
    for c in copies:
        c.start()
    for c in copies:
        c.wait()


def run_fetch(w):
    return pl.pallas_call(
        fetch_kernel,
        in_specs=[pl.BlockSpec(memory_space=pl.ANY)],
        out_specs=pl.BlockSpec(memory_space=pltpu.VMEM),
        out_shape=jax.ShapeDtypeStruct(w.shape, w.dtype),
        scratch_shapes=[pltpu.SemaphoreType.DMA((8,))],
        compiler_params=pltpu.CompilerParams(vmem_limit_bytes=LIMIT),
        name="fetch",
    )(w)


def rim_kernel(q, k, v, out_ref, sem):
    copies, at = [], 0
    for i, ref in enumerate((q, k, v)):
        rows, width = ref.shape
        copies.append(pltpu.make_async_copy(ref.at[pl.ds(rows - 8, 8)], out_ref.at[:, pl.ds(at, width)], sem.at[i]))
        at += width
    for c in copies:
        c.start()
    for c in copies:
        c.wait()


def run_rim(q, k, v):
    hbm = pl.BlockSpec(memory_space=pl.ANY)
    return pl.pallas_call(
        rim_kernel,
        in_specs=[hbm] * 3,
        out_specs=pl.BlockSpec(memory_space=pltpu.VMEM),
        out_shape=jax.ShapeDtypeStruct((8, q.shape[1] + k.shape[1] + v.shape[1]), BF16),
        scratch_shapes=[pltpu.SemaphoreType.DMA((3,))],
        compiler_params=pltpu.CompilerParams(vmem_limit_bytes=LIMIT),
        name="rim",
    )(q, k, v)


def ctx_route(dx, dz, dc):
    def dest(i):
        x, z, c = i // (Z_CHIPS * CORES), (i // CORES) % Z_CHIPS, i % CORES
        return ((x + dx) % X_CHIPS * Z_CHIPS + (z + dz) % Z_CHIPS) * CORES + (c + dc) % CORES

    return [(i, dest(i)) for i in range(X_CHIPS * Z_CHIPS * CORES)]


def mesh_route(n_ctx, heads, turns):
    pairs = [(c, h) for c in range(n_ctx) for h in range(heads)]
    return [(c * heads + h, c * heads + (h + turns[c % CORES]) % heads) for c, h in pairs]


def beside_route(n_ctx):
    flip = (Z_CHIPS * CORES, CORES)
    return [(c, c ^ flip[c % CORES]) for c in range(n_ctx)]


def shards(query_raw, key_raw, value_raw, gate_branch, gate_code, beta_code,
           conv_query, conv_key, conv_value, norm_gain, out_weight):
    ctx = lax.axis_index("ctx")
    head = lax.axis_index("head")
    heads = lax.axis_size("head")
    x, z, core = ctx // (Z_CHIPS * CORES), (ctx // CORES) % Z_CHIPS, ctx % CORES
    pos = jnp.stack([x, z, core, head]).astype(jnp.int32)
    send = lambda a, dx, dz, dc: lax.ppermute(a, "ctx", ctx_route(dx, dz, dc))
    turn = lambda a, d: lax.ppermute(a, "head", [(i, (i + d) % heads) for i in range(heads)])
    hops = (1, 3, 2)
    barrier = lax.optimization_barrier

    n_ctx = lax.axis_size("ctx")
    raws = [pltpu.with_memory_space_constraint(a, pltpu.HBM) for a in (query_raw, key_raw, value_raw)]
    halo = lax.ppermute(run_rim(*raws), "ctx", [(i, i + 1) for i in range(n_ctx - 1)])
    w_full = lax.ppermute(out_weight, ("ctx", "head"), mesh_route(n_ctx, heads, (1, 3)))
    w_near = turn(run_quarter(pos, out_weight), 2)

    base, maps, kept, away = run_scan(pos, *raws, gate_code.T, beta_code.T, halo,
                                      conv_query, conv_key, conv_value)

    line, full = (HD, 2 * HD), (Z_CHIPS, HD, 2 * HD)
    early, *both = vmem_call(pair_kernel, [full] + [line] * 4, [full], pos, kept, send(away, 0, 0, 1))
    *both, w_local = barrier((*both, out_weight))
    lines = [both[0]] + [send(both[d], 0, d, 0) for d in range(1, Z_CHIPS)]
    *lines, w_local = barrier((*lines, run_fetch(w_local)))
    pre, tot = vmem_call(prefix_kernel, [full, line], [full], pos, *lines)
    tots = [tot] + [send(tot, d, 0, 0) for d in range(1, X_CHIPS)]
    entry = vmem_call(entry_kernel, [(HD, HD)] * 4, [full, (Z_CHIPS, HD, HD)], pos, *tots, pre)
    backs = [entry[0]] + [send(entry[d], 0, d, 0) for d in range(1, Z_CHIPS)]
    own, lent = vmem_call(cores_kernel, [(Z_CHIPS, HD, HD)] * 2, [(Z_CHIPS, HD, HD)], pos, *backs, early)
    got = send(lent, 0, 0, 1)

    gain = norm_gain.reshape(1, HD)
    y_a = run_out(pos, base, maps, own, got, gate_branch, gain, 0)
    a_got = [turn(y_a[d], d) for d in hops]
    _, w_full, w_near = barrier((y_a[0], w_full, w_near))
    w_far = lax.ppermute(w_near, "ctx", beside_route(n_ctx))
    near_there, full_there = send(w_near, 0, 0, 1), send(w_full, 0, 0, 1)
    y_b = run_out(pos, base, maps, own, got, gate_branch, gain, 1)
    b_got = [turn(y_b[d], d) for d in hops]
    acc = run_own(y_a[0], y_b[0], w_local)
    acc, w_far = barrier((acc, w_far))
    far_there = send(w_far, 0, 0, 1)
    acc, w_kept = barrier((acc, w_full))
    weights = [run_fetch(w_kept), full_there, w_near, w_far, near_there, far_there]
    acc = project(pos, 0, a_got, weights, acc, False)
    return project(pos, 1, b_got, weights, acc, True)


def solution(mesh):
    return jax.shard_map(
        shards,
        mesh=mesh,
        in_specs=(P("ctx", "head"),) * 6 + (P(None, "head"),) * 3 + (P(), P("head", None)),
        out_specs=P(("ctx", "head"), None),
        check_vma=False,
    )
```
